32 devices in a mesh: member: 4 (over x, core), space: 8 (over z, y).
Axes of the slice: x: 2, y: 2, z: 4, core: 2. Of those that a mesh axis runs over, the one named last changes fastest.
Arguments:
- features: bfloat16 [4, 641, 192, 128], P('member', None, 'space'), may hold values from -6 to 6
- depth_kernel: float32 [641, 5, 5], replicated, may hold values from -1.25 to 1.25
- in_weight: bfloat16 [641, 1282], replicated, may hold values from -0.25 to 0.25
- out_weight: bfloat16 [1282, 641], replicated, may hold values from -0.15625 to 0.15625
- decoder_weight: bfloat16 [641, 72], replicated, may hold values from -0.25 to 0.25
- observed: float32 [72, 192, 128], P(None, 'space'), may hold values from -6 to 6
- land_mask: int32 [192, 128], P('space'), may hold values 0 or 1
Outputs:
- grad_features: bfloat16 [4, 641, 192, 128], P('member', None, 'space')
- decoder_grad: float32 [641, 72], replicated
The draws below stay inside these ranges and needn't reach their ends.
All inputs are finite; a program needn't handle non-finite values. No bound on the sum of `land_mask` on one device may be relied on, other than what follows from the above.
Results may differ from the reference program's by a relative error of at most 0.0054.
Values may be sent and summed in bfloat16 or wider, within the bound.
A program may use at most 128 MiB of HBM per device.

```python
import math
import jax
import jax.numpy as jnp
from jax import lax

C = 641
HID = 1282
OUT = 72
LAT = 128
MEMBERS = 4
LON = 192


def with_ends(drawn, stream_key, least, largest):
    dims = drawn.shape
    index_at = [jax.random.randint(jax.random.fold_in(stream_key, axis), (), 0, dims[axis]) for axis in range(len(dims))]
    drawn = drawn.at[tuple(index_at)].set(least)
    longest = dims.index(max(dims))
    index_at[longest] = (index_at[longest] + 1) % dims[longest]
    return drawn.at[tuple(index_at)].set(largest)


def steps_of(rng, dims, pieces, smallest, high):
    gain = 1.0
    for dim, blocks in pieces:
        heights = jax.random.uniform(jax.random.fold_in(jax.random.fold_in(rng, 6), dim), (blocks,), jnp.float32, smallest / len(pieces), high / len(pieces))
        gain = gain * jnp.repeat(jnp.exp(heights), dims[dim] // blocks).reshape((-1,) + (1,) * (len(dims) - 1 - dim))
    return gain


def noise(rng, extent, deviation, reach, cuts=(), dtype=jnp.bfloat16):
    drawn = jax.random.normal(rng, extent, jnp.float32) * deviation
    if len(cuts) > 0:
        drawn = steps_of(rng, extent, cuts, -0.22, 0.18) * drawn
    return jnp.clip(drawn, min=-reach, max=reach).astype(dtype)


def setup_inputs(seed: int = 0) -> dict:
    streams_of = jax.random.split(jax.random.key(seed), 8)
    return {
        "features": noise(streams_of[0], (MEMBERS, C, LON, LAT), 1.0, 6.0, ((0, 4), (2, 8))),
        "depth_kernel": noise(streams_of[1], (C, 5, 5), 25 ** -0.5, 1.25, (), jnp.float32),
        "in_weight": noise(streams_of[2], (C, HID), C ** -0.5, 0.25),
        "out_weight": noise(streams_of[3], (HID, C), HID ** -0.5, 0.15625),
        "decoder_weight": noise(streams_of[4], (C, OUT), C ** -0.5, 0.25),
        "observed": noise(streams_of[5], (OUT, LON, LAT), 1.0, 6.0, ((1, 8),), jnp.float32),
        "land_mask": with_ends((jax.random.randint(streams_of[6], (LON, LAT), 0, 10) < 3).astype(jnp.int32), jax.random.fold_in(streams_of[6], 1), 0, 1),
    }


norm_eps = 1e-05

def convolve(field, depth_kernel):
    lat_len = field.shape[2]
    widened = jnp.pad(field.astype(jnp.float32), ((0, 0), (0, 0), (2, 2)))
    total = jnp.zeros(field.shape, jnp.float32)
    for row_off in range(5):
        rolled = jnp.roll(widened, 2 - row_off, axis=1)
        for col_off in range(5):
            total = total + depth_kernel[:, row_off, col_off][:, None, None] * rolled[:, :, col_off:col_off + lat_len]
    return total

def forward(field, depth_kernel, in_weight, out_weight, decoder_weight):
    channels = field.shape[0]
    convolved = convolve(field, depth_kernel)
    center = lax.optimization_barrier(jnp.mean(convolved, axis=0, keepdims=True))
    shifted = convolved - center
    normed = (shifted * lax.rsqrt(lax.optimization_barrier(jnp.mean(shifted * shifted, axis=0, keepdims=True)) + norm_eps)).astype(jnp.bfloat16)
    flat = normed.reshape(channels, -1)
    hidden = jax.nn.gelu(jnp.dot(in_weight.T, flat, preferred_element_type=jnp.float32), approximate=False).astype(jnp.bfloat16)
    mlp_out = jnp.dot(out_weight.T, hidden, preferred_element_type=jnp.float32)
    block_out = (field.reshape(channels, -1).astype(jnp.float32) + mlp_out).astype(jnp.bfloat16)
    decoded = jnp.dot(decoder_weight.T, block_out, preferred_element_type=jnp.float32).astype(jnp.bfloat16)
    return (block_out, decoded)

def reference(features, depth_kernel, in_weight, out_weight, decoder_weight, observed, land_mask):
    members = features.shape[0]
    channels = features.shape[1]
    points = features.shape[2] * features.shape[3]
    block_out, decoded = lax.map(lambda field: forward(field, depth_kernel, in_weight, out_weight, decoder_weight), features)
    decoded_f = decoded.astype(jnp.float32)
    obs_flat = observed.reshape(observed.shape[0], -1)
    point_weight = (4.0 + 8.0 * land_mask.astype(jnp.float32)).reshape(-1)
    misfit = decoded_f - obs_flat[None]
    misfit_norm = jnp.sqrt(lax.optimization_barrier(jnp.sum(misfit * misfit, axis=1, keepdims=True)) + 1.0)

    def add_pair(other, total):
        apart = decoded_f - lax.dynamic_index_in_dim(decoded_f, other, 0, True)
        return total + apart / jnp.sqrt(lax.optimization_barrier(jnp.sum(apart * apart, axis=1, keepdims=True)) + 1.0)
    pair_sum = lax.fori_loop(0, members, add_pair, jnp.zeros(decoded_f.shape, jnp.float32))
    score_grad = (point_weight[None, None, :] * (misfit / misfit_norm - pair_sum / members)).astype(jnp.bfloat16)
    grad_flat = lax.map(lambda grad_one: jnp.dot(decoder_weight, grad_one, preferred_element_type=jnp.float32).astype(jnp.bfloat16), score_grad)
    grad_features = grad_flat.reshape(features.shape)

    def add_term(total, pair):
        return (total + jnp.dot(pair[0], pair[1].T, preferred_element_type=jnp.float32), None)
    summed, _ = lax.scan(add_term, jnp.zeros((channels, decoder_weight.shape[1]), jnp.float32), (block_out, score_grad))
    decoder_grad = summed / math.sqrt(members * points)
    return (grad_features, decoder_grad)
```

```python
import functools
import math

import jax
import jax.numpy as jnp
from jax import lax
from jax.experimental import pallas as pl
from jax.experimental.pallas import tpu as pltpu
from jax.sharding import PartitionSpec as P

norm_eps = 1e-05
MESH = pl.DeviceIdType.MESH
VMEM_SPEC = pl.BlockSpec(memory_space=pltpu.VMEM)
ANY_SPEC = pl.BlockSpec(memory_space=pl.ANY)
f32 = jnp.float32
bf16 = jnp.bfloat16


def round_up(value, step):
    return -(-value // step) * step


def spans(total, width):
    return [(at, min(at + width, total)) for at in range(0, total, width)]


def gelu(x):
    return 0.5 * x * (1.0 + lax.erf(x * (0.5**0.5)))


def pair_tree(terms):
    while len(terms) > 1:
        terms = [
            terms[i] + terms[i + 1] if i + 1 < len(terms) else terms[i]
            for i in range(0, len(terms), 2)
        ]
    return terms[0]


def interleave(main, side):
    total = sum(share for _, share in main)
    done = 0
    given = 0.0
    for piece, share in main:
        piece()
        given += share
        until = len(side) if given >= total else int(round(len(side) * given / total))
        while done < until:
            side[done]()
            done += 1


def kernel(
    groups, half, scale, x_hbm, taps_hbm, w1_hbm, w2_hbm, dect_hbm, observed_hbm, mask_hbm, grad_hbm, out_ref,
    x_ref, plane_ref, taps_in, tin_ref, taps_ref, w1n_ref, w1_ref, w2_ref, dect_ref, dec_ref, observed_ref, mask_ref,
    conv_ref, normed_ref, act_ref, block_ref, own_ref, others_ref, score_ref, tall_ref, term_ref, mine, got,
    mine_sum, whole, edge_out, edge_in, load_sems, x_sems, halo_sems, pair_sems, sems,
):
    channels, lon_len, lat_len = x_ref.shape
    hid = w1_ref.shape[0]
    size = 2 * half + 1
    pitch = plane_ref.shape[0] // (lon_len + 2 * half)
    rows = 2 * half
    steps = lon_len // rows
    member_n, space_n = groups
    n = member_n * space_n
    member = lax.axis_index("member")
    space = lax.axis_index("space")
    me = member * space_n + space

    def peer(e):
        other = lax.rem(me + e + 1, n)
        return other, (other // space_n, lax.rem(other, space_n))

    barrier = pltpu.get_barrier_semaphore()

    def greet(e, carry):
        pl.semaphore_signal(barrier, inc=1, device_id=peer(e)[1], device_id_type=MESH)
        return carry

    loads = [
        pltpu.make_async_copy(src, dst, load_sems.at[k])
        for k, (src, dst) in enumerate(
            (
                (w1_hbm, w1n_ref), (taps_hbm, taps_in), (w2_hbm, w2_ref), (dect_hbm, dect_ref),
                (observed_hbm, observed_ref), (mask_hbm, mask_ref),
            )
        )
    ]
    ends = [128 * k for k in range(1, channels // 128)] + [channels]
    parts = list(zip([0] + ends[:-1], ends))
    x_loads = [
        pltpu.make_async_copy(x_hbm.at[low:high], x_ref.at[low:high], x_sems.at[k])
        for k, (low, high) in enumerate(parts)
    ]
    loads[0].start()
    loads[1].start()
    for copy in x_loads:
        copy.start()
    for copy in loads[2:]:
        copy.start()
    lax.fori_loop(0, n - 1, greet, 0)

    loads[1].wait()
    tin_ref[...] = jnp.zeros_like(tin_ref)
    for p in range(size):
        tin_ref[size * p : size * (p + 1), 0:channels] = taps_in[p]
    taps_ref[...] = jnp.transpose(tin_ref[...])
    spare = pitch - channels
    for r in range(lon_len + 2 * half):
        plane_ref[r * pitch + channels : (r + 1) * pitch, :] = jnp.zeros((spare, lat_len), f32)
    loads[0].wait()
    for low, high in spans(hid, 256):
        w1_ref[low:high, :] = jnp.transpose(w1n_ref[:, low:high])

    def turn(c):
        plane_ref[pl.ds(half * pitch + c, lon_len, stride=pitch), :] = x_ref[c].astype(f32)

    def turn8(i, carry):
        for k in range(8):
            turn(i * 8 + k)
        return carry

    for k, (low, high) in enumerate(parts):
        x_loads[k].wait()
        lax.fori_loop(low // 8, high // 8, turn8, 0)
        for c in range(high // 8 * 8, high):
            turn(c)

    lane = lax.broadcasted_iota(jnp.int32, (16, lat_len), 1)
    inside = []
    for q in range(size):
        shift = half - q
        if shift == 0:
            inside.append(None)
        else:
            ok = lane >= shift if shift > 0 else lane < lat_len + shift
            inside.append(jnp.where(ok, 1.0, 0.0).astype(bf16))

    def conv_chunk(first, runs):
        tap = taps_ref[pl.ds(first, 16), :].astype(bf16)
        coef = []
        for p in range(size):
            for q in range(size):
                at = p * size + q
                wide = jnp.broadcast_to(tap[:, at : at + 1], (16, lat_len))
                coef.append(wide if inside[q] is None else wide * inside[q])
        for base, count, slot in runs:
            acc = [None] * count
            for k in range(count + 2 * half):
                cell = plane_ref[pl.ds((base + k) * pitch + first, 16), :].astype(bf16)
                moved = [
                    cell if q == half else pltpu.roll(cell, (half - q) % lat_len, 1) for q in range(size)
                ]
                for o in range(count):
                    p = k - o
                    if 0 <= p < size:
                        part = pair_tree([coef[p * size + q] * moved[q] for q in range(size)]).astype(f32)
                        acc[o] = part if acc[o] is None else acc[o] + part
            for o in range(count):
                conv_ref[slot + o, pl.ds(first, 16), :] = acc[o]

    chunks = -(-channels // 16)

    def conv_pieces(runs):
        return [functools.partial(conv_chunk, 16 * k, runs) for k in range(chunks)]

    def norm_row(r):
        cells = conv_ref[r, 0:channels, :]
        shifted = cells - jnp.sum(cells, axis=0, keepdims=True) * (1.0 / channels)
        square = jnp.sum(shifted * shifted, axis=0, keepdims=True)
        factor = lax.rsqrt(square * (1.0 / channels) + norm_eps)
        normed_ref[:, r * lat_len : (r + 1) * lat_len] = (shifted * factor).astype(bf16)

    def pre_piece(low, high):
        pre = jnp.dot(w1_ref[low:high, :], normed_ref[...], preferred_element_type=f32)
        act_ref[low:high, :] = gelu(pre).astype(bf16)

    def out_piece(step, lons, low, high):
        held = jnp.concatenate(
            [plane_ref[pl.ds((lon + half) * pitch + low, high - low), :] for lon in lons], axis=1
        )
        out = held + jnp.dot(w2_ref[low:high, :], act_ref[...], preferred_element_type=f32)
        block_ref[step, low:high, :] = out.astype(bf16)

    def decode_piece(step):
        decoded = jnp.dot(dect_ref[...], block_ref[step], preferred_element_type=f32).astype(bf16)
        for r in range(rows):
            own_ref[step * rows + r] = decoded[:, r * lat_len : (r + 1) * lat_len]

    def mlp_pieces(step, lons):
        first = [
            (functools.partial(pre_piece, low, high), 3.0 * (high - low) / 256) for low, high in spans(hid, 256)
        ]
        second = [
            (functools.partial(out_piece, step, lons, low, high), 11.0 * (high - low) / 256)
            for low, high in spans(channels, 256)
        ]
        return first + second

    def fused(step, lons, runs):
        interleave(mlp_pieces(step, lons), conv_pieces(runs))
        decode_piece(step)
        for r in range(rows):
            norm_row(r)

    def pair_copy(step, j):
        at = pl.ds(step * rows, rows)
        return pltpu.make_async_remote_copy(
            src_ref=own_ref.at[at], dst_ref=others_ref.at[j, at],
            send_sem=pair_sems.at[0, j, step], recv_sem=pair_sems.at[1, j, step],
            device_id=(lax.rem(member + j + 1, member_n), space), device_id_type=MESH,
        )

    def send_pairs(step):
        for j in range(member_n - 1):
            pair_copy(step, j).start()

    def halo_copy(side):
        to = lax.rem(space + (space_n - 1 if side == 0 else 1), space_n)
        return pltpu.make_async_remote_copy(
            src_ref=edge_out.at[side], dst_ref=edge_in.at[side], send_sem=halo_sems.at[0, side],
            recv_sem=halo_sems.at[1, side], device_id=(member, to), device_id_type=MESH,
        )

    padded = edge_out.shape[2]
    for r in range(half):
        edge_out[0, r] = plane_ref[(half + r) * pitch : (half + r) * pitch + padded, :].astype(bf16)
        edge_out[1, r] = plane_ref[(lon_len + r) * pitch : (lon_len + r) * pitch + padded, :].astype(bf16)

    def conv_loop(k, carry):
        conv_chunk(pl.multiple_of(k * 16, 16), [(half, rows, 0)])
        return carry

    lax.fori_loop(0, chunks, conv_loop, 0)
    for r in range(rows):
        norm_row(r)
    pl.semaphore_wait(barrier, n - 1)
    for side in range(2):
        halo_copy(side).start()
    for copy in loads[2:]:
        copy.wait()
    dec_ref[...] = jnp.transpose(dect_ref[...])

    def lons_of(step):
        return [half + step * rows + r for r in range(rows)]

    def main_loop(step, carry):
        fused(step, lons_of(step), [(half + (step + 1) * rows, rows, 0)])
        send_pairs(step)
        return carry

    lax.fori_loop(0, steps - 2, main_loop, 0)
    for side in range(2):
        halo_copy(side).wait()
    for r in range(half):
        top = (lon_len + half + r) * pitch
        plane_ref[top : top + padded, :] = edge_in[0, r].astype(f32)
        plane_ref[r * pitch : r * pitch + padded, :] = edge_in[1, r].astype(f32)
    fused(steps - 2, lons_of(steps - 2), [(0, half, 0), (lon_len - half, half, half)])
    send_pairs(steps - 2)
    outer = list(range(half)) + list(range(lon_len - half, lon_len))
    for piece, _ in mlp_pieces(steps - 1, outer):
        piece()
    decode_piece(steps - 1)
    send_pairs(steps - 1)

    tall_ref[...] = jnp.zeros_like(tall_ref)
    term_ref[...] = jnp.zeros_like(term_ref)

    def score_row(step, r, lon):
        at = step * rows + r
        own = own_ref[at].astype(f32)
        misfit = own - observed_ref[pl.ds(lon, own.shape[0], stride=lon_len), :]
        total = misfit * lax.rsqrt(jnp.sum(misfit * misfit, axis=0, keepdims=True) + 1.0)
        pair_sum = jnp.zeros_like(own)
        for k in range(member_n):
            other = own_ref[at] if k == member_n - 1 else others_ref[k, at]
            apart = own - other.astype(f32)
            pair_sum = pair_sum + apart * lax.rsqrt(jnp.sum(apart * apart, axis=0, keepdims=True) + 1.0)
        weight = 4.0 + 8.0 * mask_ref[pl.ds(lon, 1), :].astype(f32)
        score_ref[step, :, r * lat_len : (r + 1) * lat_len] = (
            weight * (total - pair_sum / member_n)
        ).astype(bf16)

    def score_step(step, lons):
        for j in range(member_n - 1):
            pair_copy(step, j).wait()
        for r in range(rows):
            score_row(step, r, lons[r])
        tall_ref[...] += lax.dot_general(
            block_ref[step], score_ref[step], (((1,), (1,)), ((), ())), preferred_element_type=f32
        )

    def score_loop(step, carry):
        score_step(step, lons_of(step))
        return carry

    lax.fori_loop(0, steps - 1, score_loop, 0)
    score_step(steps - 1, outer)
    term_ref[:, 0:channels] = scale * jnp.transpose(tall_ref[...])

    per = mine_sum.shape[0] // 8
    tall = term_ref.shape[0] // 8
    across = term_ref.shape[1] // 128
    for a in range(tall):
        for b in range(across):
            at = a * across + b
            low = 8 * (at % per)
            mine[at // per, low : low + 8, :] = term_ref[
                8 * a : 8 * a + 8, 128 * b : 128 * b + 128
            ].astype(bf16)
    for at in range(tall * across, n * per):
        low = 8 * (at % per)
        mine[at // per, low : low + 8, :] = jnp.zeros((8, 128), bf16)

    def scatter_copy(e):
        other, device = peer(e)
        return pltpu.make_async_remote_copy(
            src_ref=mine.at[other], dst_ref=got.at[e], send_sem=sems.at[0, e],
            recv_sem=sems.at[1, e], device_id=device, device_id_type=MESH,
        )

    def gather_copy(e):
        _, device = peer(e)
        return pltpu.make_async_remote_copy(
            src_ref=mine_sum, dst_ref=whole.at[e], send_sem=sems.at[2, e],
            recv_sem=sems.at[3, e], device_id=device, device_id_type=MESH,
        )

    def start(make):
        def body(e, carry):
            make(e).start()
            return carry

        lax.fori_loop(0, n - 1, body, 0)

    def finish(make):
        def body(e, carry):
            make(e).wait()
            return carry

        lax.fori_loop(0, n - 1, body, 0)

    start(scatter_copy)

    def grad_step(step, lons):
        grad = jnp.dot(dec_ref[...], score_ref[step], preferred_element_type=f32)
        for r in range(rows):
            plane_ref[pl.ds(lons[r] * pitch, channels), :] = grad[:, r * lat_len : (r + 1) * lat_len]

    def grad_loop(step, carry):
        grad_step(step, lons_of(step))
        return carry

    lax.fori_loop(0, steps - 1, grad_loop, 0)
    grad_step(steps - 1, outer)

    def turn_back(c):
        x_ref[c] = plane_ref[pl.ds(c, lon_len, stride=pitch), :].astype(bf16)

    def turn_back8(i, carry):
        for k in range(8):
            turn_back(i * 8 + k)
        return carry

    def store_part(k):
        low, high = parts[k]
        return pltpu.make_async_copy(x_ref.at[low:high], grad_hbm.at[low:high], x_sems.at[k])

    def turn_part(k):
        low, high = parts[k]
        lax.fori_loop(low // 8, high // 8, turn_back8, 0)
        for c in range(high // 8 * 8, high):
            turn_back(c)
        store_part(k).start()

    middle = len(parts) // 2
    for k in range(middle):
        turn_part(k)
    finish(scatter_copy)
    total = mine[me].astype(f32)
    for e in range(n - 1):
        total = total + got[e].astype(f32)
    mine_sum[...] = total.astype(bf16)
    start(gather_copy)
    out_ref[me] = mine_sum[...].astype(f32)
    for k in range(middle, len(parts)):
        turn_part(k)
    finish(gather_copy)
    for e in range(n - 1):
        out_ref[lax.rem(me + n - e - 1, n)] = whole[e].astype(f32)
    for k in range(len(parts)):
        store_part(k).wait()


def per_device(features, depth_kernel, in_weight, out_weight, decoder_weight, observed, land_mask):
    _, channels, lon_len, lat_len = features.shape
    hid = in_weight.shape[1]
    outputs = decoder_weight.shape[1]
    size = depth_kernel.shape[1]
    half = size // 2
    member_n = lax.axis_size("member")
    space_n = lax.axis_size("space")
    n = member_n * space_n
    members = features.shape[0] * member_n
    total_points = lon_len * space_n * lat_len
    padded_c = round_up(channels, 16)
    pitch = padded_c + 1
    wide_c = round_up(channels, 128)
    tiles = (outputs // 8) * (wide_c // 128)
    per = -(-tiles // n)
    rows = 2 * half
    steps = lon_len // rows
    wide = rows * lat_len
    parts = channels // 128
    grad, summed = pl.pallas_call(
        functools.partial(kernel, (member_n, space_n), half, 1.0 / math.sqrt(members * total_points)),
        name="main",
        out_shape=(
            jax.ShapeDtypeStruct((channels, lon_len, lat_len), bf16),
            jax.ShapeDtypeStruct((n, per * 8, 128), f32),
        ),
        in_specs=[ANY_SPEC] * 7,
        out_specs=[ANY_SPEC, VMEM_SPEC],
        scratch_shapes=[
            pltpu.VMEM((channels, lon_len, lat_len), bf16),
            pltpu.VMEM(((lon_len + 2 * half) * pitch, lat_len), f32),
            pltpu.VMEM((size, size, channels), f32),
            pltpu.VMEM((round_up(size * size, 32), wide_c), f32),
            pltpu.VMEM((wide_c, round_up(size * size, 32)), f32),
            pltpu.VMEM((channels, hid), bf16),
            pltpu.VMEM((hid, channels), bf16),
            pltpu.VMEM((channels, hid), bf16),
            pltpu.VMEM((outputs, channels), bf16),
            pltpu.VMEM((channels, outputs), bf16),
            pltpu.VMEM((outputs * lon_len, lat_len), f32),
            pltpu.VMEM((lon_len, lat_len), jnp.int32),
            pltpu.VMEM((rows, padded_c, lat_len), f32),
            pltpu.VMEM((channels, wide), bf16),
            pltpu.VMEM((hid, wide), bf16),
            pltpu.VMEM((steps, channels, wide), bf16),
            pltpu.VMEM((lon_len, outputs, lat_len), bf16),
            pltpu.VMEM((member_n - 1, lon_len, outputs, lat_len), bf16),
            pltpu.VMEM((steps, outputs, wide), bf16),
            pltpu.VMEM((channels, outputs), f32),
            pltpu.VMEM((outputs, wide_c), f32),
            pltpu.VMEM((n, per * 8, 128), bf16),
            pltpu.VMEM((n - 1, per * 8, 128), bf16),
            pltpu.VMEM((per * 8, 128), bf16),
            pltpu.VMEM((n - 1, per * 8, 128), bf16),
            pltpu.VMEM((2, half, padded_c, lat_len), bf16),
            pltpu.VMEM((2, half, padded_c, lat_len), bf16),
            pltpu.SemaphoreType.DMA((6,)),
            pltpu.SemaphoreType.DMA((parts,)),
            pltpu.SemaphoreType.DMA((2, 2)),
            pltpu.SemaphoreType.DMA((2, member_n - 1, steps)),
            pltpu.SemaphoreType.DMA((4, n - 1)),
        ],
        compiler_params=pltpu.CompilerParams(
            collective_id=0, has_side_effects=True, vmem_limit_bytes=56 * 1024 * 1024
        ),
    )(
        features[0], jnp.transpose(depth_kernel, (1, 2, 0)), in_weight, out_weight.T, decoder_weight.T,
        observed.reshape(outputs * lon_len, lat_len), land_mask,
    )
    flat = summed.reshape(n * per, 8, 128)[:tiles].reshape(outputs // 8, wide_c // 128, 8, 128)
    decoder_grad = jnp.transpose(flat, (0, 2, 1, 3)).reshape(outputs, wide_c)[:, :channels].T
    return (grad[None], decoder_grad)


def solution(mesh):
    placed = (
        P("member", None, "space", None),
        P(),
        P(),
        P(),
        P(),
        P(None, "space", None),
        P("space", None),
    )
    return jax.shard_map(
        per_device,
        mesh=mesh,
        in_specs=placed,
        out_specs=(P("member", None, "space", None), P()),
        check_vma=False,
    )
```

```python
import functools
import math

import jax
import jax.numpy as jnp
from jax import lax
from jax.experimental import pallas as pl
from jax.experimental.pallas import tpu as pltpu
from jax.sharding import PartitionSpec as P

norm_eps = 1e-05
MESH = pl.DeviceIdType.MESH
VMEM_SPEC = pl.BlockSpec(memory_space=pltpu.VMEM)
ANY_SPEC = pl.BlockSpec(memory_space=pl.ANY)
f32 = jnp.float32
bf16 = jnp.bfloat16


def round_up(value, step):
    return -(-value // step) * step


def spans(total, width):
    return [(at, min(at + width, total)) for at in range(0, total, width)]


def gelu_of_half(u):
    return u * (1.0 + lax.erf(u * (2.0**0.5)))


def pair_tree(terms):
    while len(terms) > 1:
        terms = [
            terms[i] + terms[i + 1] if i + 1 < len(terms) else terms[i]
            for i in range(0, len(terms), 2)
        ]
    return terms[0]


def interleave(main, side):
    total = sum(share for _, share in main)
    done = 0
    given = 0.0
    for piece, share in main:
        piece()
        given += share
        until = len(side) if given >= total else int(round(len(side) * given / total))
        while done < until:
            side[done]()
            done += 1


def kernel(
    groups, half, scale, x_hbm, taps_hbm, w1_hbm, w2_hbm, dect_hbm, observed_hbm, mask_hbm, grad_ref, out_ref,
    x_ref, plane_ref, taps_in, tin_ref, taps_ref, coef_ref, w1n_ref, w1_ref, w2_ref, dect_ref, dec_ref, observed_ref, mask_ref,
    conv_ref, normed_ref, act_ref, block_ref, own_ref, others_ref, score_ref, tall_ref, term_ref, mine, got,
    mine_sum, whole, edge_out, edge_in, load_sems, x_sems, halo_sems, pair_sems, sems,
):
    channels, lon_len, lat_len = x_ref.shape
    hid = w1_ref.shape[0]
    size = 2 * half + 1
    pitch = plane_ref.shape[0] // (lon_len + 2 * half)
    rows = 2 * half
    steps = lon_len // rows
    member_n, space_n = groups
    n = member_n * space_n
    member = lax.axis_index("member")
    space = lax.axis_index("space")
    me = member * space_n + space

    def peer(e):
        other = lax.rem(me + e + 1, n)
        return other, (other // space_n, lax.rem(other, space_n))

    barrier = pltpu.get_barrier_semaphore()

    def greet(e, carry):
        pl.semaphore_signal(barrier, inc=1, device_id=peer(e)[1], device_id_type=MESH)
        return carry

    loads = [
        pltpu.make_async_copy(src, dst, load_sems.at[k])
        for k, (src, dst) in enumerate(
            (
                (w1_hbm, w1n_ref), (taps_hbm, taps_in), (w2_hbm, w2_ref), (dect_hbm, dect_ref),
                (observed_hbm, observed_ref), (mask_hbm, mask_ref),
            )
        )
    ]
    ends = [128 * k for k in range(1, channels // 128)] + [channels]
    parts = list(zip([0] + ends[:-1], ends))
    x_loads = [
        pltpu.make_async_copy(x_hbm.at[low:high], x_ref.at[low:high], x_sems.at[k])
        for k, (low, high) in enumerate(parts)
    ]
    loads[1].start()
    loads[0].start()
    for copy in x_loads:
        copy.start()
    for copy in loads[2:]:
        copy.start()
    lax.fori_loop(0, n - 1, greet, 0)

    loads[1].wait()
    tin_ref[...] = jnp.zeros_like(tin_ref)
    for p in range(size):
        tin_ref[size * p : size * (p + 1), 0:channels] = taps_in[p]
    taps_ref[...] = jnp.transpose(tin_ref[...])
    lane = lax.broadcasted_iota(jnp.int32, (16, lat_len), 1)
    inside = []
    for q in range(size):
        shift = half - q
        if shift == 0:
            inside.append(None)
        else:
            ok = lane >= shift if shift > 0 else lane < lat_len + shift
            inside.append(jnp.where(ok, 1.0, 0.0).astype(bf16))

    chunks = -(-channels // 16)

    def spread(k, carry):
        here = pl.ds(pl.multiple_of(k * 16, 16), 16)
        tap = taps_ref[here, :].astype(bf16)
        for at in range(size * size):
            wide = jnp.broadcast_to(tap[:, at : at + 1], (16, lat_len))
            mask = inside[at % size]
            coef_ref[at, here, :] = (wide if mask is None else wide * mask).astype(f32)
        return carry

    lax.fori_loop(0, chunks, spread, 0)
    spare = pitch - channels
    for r in range(lon_len + 2 * half):
        plane_ref[r * pitch + channels : (r + 1) * pitch, :] = jnp.zeros((spare, lat_len), f32)
    loads[0].wait()
    for low, high in spans(hid, 256):
        w1_ref[low:high, :] = jnp.transpose(w1n_ref[:, low:high])

    def turn(c):
        plane_ref[pl.ds(half * pitch + c, lon_len, stride=pitch), :] = x_ref[c].astype(f32)

    def turn8(i, carry):
        for k in range(8):
            turn(i * 8 + k)
        return carry

    for k, (low, high) in enumerate(parts):
        x_loads[k].wait()
        lax.fori_loop(low // 8, high // 8, turn8, 0)
        for c in range(high // 8 * 8, high):
            turn(c)

    def conv_chunk(first, runs):
        cells = {}
        sums = {}
        for base, count, slot in runs:
            for k in range(count + 2 * half):
                cells[slot, k] = plane_ref[pl.ds((base + k) * pitch + first, 16), :].astype(bf16)
        for q in range(size):
            coef = [coef_ref[p * size + q, pl.ds(first, 16), :].astype(bf16) for p in range(size)]
            for base, count, slot in runs:
                moved = [
                    cells[slot, k] if q == half else pltpu.roll(cells[slot, k], (half - q) % lat_len, 1)
                    for k in range(count + 2 * half)
                ]
                for o in range(count):
                    part = pair_tree([coef[p] * moved[o + p] for p in range(size)])
                    sums.setdefault(slot + o, []).append(part)
        for o, terms in sums.items():
            conv_ref[o, pl.ds(first, 16), :] = pair_tree(terms).astype(f32)

    def conv_pieces(runs):
        return [functools.partial(conv_chunk, 16 * k, runs) for k in range(chunks)]

    def norm_row(r):
        cells = conv_ref[r, 0:channels, :]
        shifted = cells - jnp.sum(cells, axis=0, keepdims=True) * (1.0 / channels)
        square = jnp.sum(shifted * shifted, axis=0, keepdims=True)
        factor = 0.5 * lax.rsqrt(square * (1.0 / channels) + norm_eps)
        normed_ref[:, r * lat_len : (r + 1) * lat_len] = (shifted * factor).astype(bf16)

    def pre_piece():
        pre = jnp.dot(w1_ref[...], normed_ref[...], preferred_element_type=f32)
        act_ref[...] = gelu_of_half(pre).astype(bf16)

    def out_piece(step, lons):
        held = jnp.concatenate([plane_ref[pl.ds((lon + half) * pitch, channels), :] for lon in lons], axis=1)
        out = held + jnp.dot(w2_ref[...], act_ref[...], preferred_element_type=f32)
        block_ref[step] = out.astype(bf16)

    def decode_piece(step):
        decoded = jnp.dot(dect_ref[...], block_ref[step], preferred_element_type=f32).astype(bf16)
        for r in range(rows):
            own_ref[step * rows + r] = decoded[:, r * lat_len : (r + 1) * lat_len]

    def mlp_pieces(step, lons):
        return [
            (pre_piece, 15.0), (functools.partial(out_piece, step, lons), 27.0),
            (functools.partial(decode_piece, step), 1.0),
        ]

    def fused(step, lons, runs):
        norms = [functools.partial(norm_row, r) for r in range(rows)]
        interleave(mlp_pieces(step, lons), conv_pieces(runs) + norms)

    def pair_copy(step, j):
        at = pl.ds(step * rows, rows)
        return pltpu.make_async_remote_copy(
            src_ref=own_ref.at[at], dst_ref=others_ref.at[j, at],
            send_sem=pair_sems.at[0, j, step], recv_sem=pair_sems.at[1, j, step],
            device_id=(lax.rem(member + j + 1, member_n), space), device_id_type=MESH,
        )

    def send_pairs(step):
        for j in range(member_n - 1):
            pair_copy(step, j).start()

    def halo_copy(side):
        to = lax.rem(space + (space_n - 1 if side == 0 else 1), space_n)
        return pltpu.make_async_remote_copy(
            src_ref=edge_out.at[side], dst_ref=edge_in.at[side], send_sem=halo_sems.at[0, side],
            recv_sem=halo_sems.at[1, side], device_id=(member, to), device_id_type=MESH,
        )

    padded = edge_out.shape[2]
    for r in range(half):
        edge_out[0, r] = plane_ref[(half + r) * pitch : (half + r) * pitch + padded, :].astype(bf16)
        edge_out[1, r] = plane_ref[(lon_len + r) * pitch : (lon_len + r) * pitch + padded, :].astype(bf16)

    def conv_loop(k, carry):
        for part in range(2):
            conv_chunk(pl.multiple_of(k * 32 + 16 * part, 16), [(half, rows, 0)])
        return carry

    lax.fori_loop(0, chunks // 2, conv_loop, 0)
    if chunks % 2:
        conv_chunk(16 * chunks - 16, [(half, rows, 0)])
    for r in range(rows):
        norm_row(r)
    pl.semaphore_wait(barrier, n - 1)
    for side in range(2):
        halo_copy(side).start()
    for copy in loads[2:]:
        copy.wait()
    dec_ref[...] = jnp.transpose(dect_ref[...])

    def lons_of(step):
        return [half + step * rows + r for r in range(rows)]

    def main_loop(step, carry):
        fused(step, lons_of(step), [(half + (step + 1) * rows, rows, 0)])
        send_pairs(step)
        return carry

    lax.fori_loop(0, steps - 2, main_loop, 0)
    for side in range(2):
        halo_copy(side).wait()
    for r in range(half):
        top = (lon_len + half + r) * pitch
        plane_ref[top : top + padded, :] = edge_in[0, r].astype(f32)
        plane_ref[r * pitch : r * pitch + padded, :] = edge_in[1, r].astype(f32)
    fused(steps - 2, lons_of(steps - 2), [(0, half, 0), (lon_len - half, half, half)])
    send_pairs(steps - 2)
    outer = list(range(half)) + list(range(lon_len - half, lon_len))
    for piece, _ in mlp_pieces(steps - 1, outer):
        piece()
    send_pairs(steps - 1)

    tall_ref[...] = jnp.zeros_like(tall_ref)
    term_ref[...] = jnp.zeros_like(term_ref)

    def score_row(step, r, lon):
        at = step * rows + r
        own = own_ref[at].astype(f32)
        misfit = own - observed_ref[pl.ds(lon, own.shape[0], stride=lon_len), :]
        total = misfit * lax.rsqrt(jnp.sum(misfit * misfit, axis=0, keepdims=True) + 1.0)
        pair_sum = jnp.zeros_like(own)
        for k in range(member_n):
            other = own_ref[at] if k == member_n - 1 else others_ref[k, at]
            apart = own - other.astype(f32)
            pair_sum = pair_sum + apart * lax.rsqrt(jnp.sum(apart * apart, axis=0, keepdims=True) + 1.0)
        weight = 4.0 + 8.0 * mask_ref[pl.ds(lon, 1), :].astype(f32)
        score_ref[step, :, r * lat_len : (r + 1) * lat_len] = (
            weight * (total - pair_sum / member_n)
        ).astype(bf16)

    def score_step(step, lons):
        for j in range(member_n - 1):
            pair_copy(step, j).wait()
        for r in range(rows):
            score_row(step, r, lons[r])
        tall_ref[...] += lax.dot_general(
            block_ref[step], score_ref[step], (((1,), (1,)), ((), ())), preferred_element_type=f32
        )

    def score_loop(step, carry):
        score_step(step, lons_of(step))
        return carry

    lax.fori_loop(0, steps - 1, score_loop, 0)
    score_step(steps - 1, outer)
    term_ref[:, 0:channels] = scale * jnp.transpose(tall_ref[...])

    per = mine_sum.shape[0] // 8
    tall = term_ref.shape[0] // 8
    across = term_ref.shape[1] // 128
    for a in range(tall):
        for b in range(across):
            at = a * across + b
            low = 8 * (at % per)
            mine[at // per, low : low + 8, :] = term_ref[
                8 * a : 8 * a + 8, 128 * b : 128 * b + 128
            ].astype(bf16)
    for at in range(tall * across, n * per):
        low = 8 * (at % per)
        mine[at // per, low : low + 8, :] = jnp.zeros((8, 128), bf16)

    def scatter_copy(e):
        other, device = peer(e)
        return pltpu.make_async_remote_copy(
            src_ref=mine.at[other], dst_ref=got.at[e], send_sem=sems.at[0, e],
            recv_sem=sems.at[1, e], device_id=device, device_id_type=MESH,
        )

    def gather_copy(e):
        _, device = peer(e)
        return pltpu.make_async_remote_copy(
            src_ref=mine_sum, dst_ref=whole.at[e], send_sem=sems.at[2, e],
            recv_sem=sems.at[3, e], device_id=device, device_id_type=MESH,
        )

    def start(make):
        def body(e, carry):
            make(e).start()
            return carry

        lax.fori_loop(0, n - 1, body, 0)

    def finish(make):
        def body(e, carry):
            make(e).wait()
            return carry

        lax.fori_loop(0, n - 1, body, 0)

    start(scatter_copy)

    def grad_step(step, lons):
        grad = jnp.dot(dec_ref[...], score_ref[step], preferred_element_type=f32)
        for r in range(rows):
            plane_ref[pl.ds(lons[r] * pitch, channels), :] = grad[:, r * lat_len : (r + 1) * lat_len]

    def grad_loop(step, carry):
        grad_step(step, lons_of(step))
        return carry

    lax.fori_loop(0, steps - 1, grad_loop, 0)
    grad_step(steps - 1, outer)

    def turn_back(c):
        grad_ref[c] = plane_ref[pl.ds(c, lon_len, stride=pitch), :].astype(bf16)

    def turn_back8(i, carry):
        for k in range(8):
            turn_back(i * 8 + k)
        return carry

    def turn_part(k):
        low, high = parts[k]
        lax.fori_loop(low // 8, high // 8, turn_back8, 0)
        for c in range(high // 8 * 8, high):
            turn_back(c)

    middle = len(parts) // 2
    for k in range(middle):
        turn_part(k)
    finish(scatter_copy)
    total = mine[me].astype(f32)
    for e in range(n - 1):
        total = total + got[e].astype(f32)
    mine_sum[...] = total.astype(bf16)
    start(gather_copy)
    out_ref[me] = mine_sum[...].astype(f32)
    for k in range(middle, len(parts)):
        turn_part(k)
    finish(gather_copy)
    for e in range(n - 1):
        out_ref[lax.rem(me + n - e - 1, n)] = whole[e].astype(f32)

def last_kernel(grad_in, tiles_ref, grad_out, out_ref, flat_ref, sems):
    channels = grad_in.shape[0]
    parts = spans(channels, 128)
    copies = [
        pltpu.make_async_copy(grad_in.at[low:high], grad_out.at[low:high], sems.at[k])
        for k, (low, high) in enumerate(parts)
    ]
    for copy in copies:
        copy.start()
    across = flat_ref.shape[1] // 128
    per = tiles_ref.shape[1] // 8
    for at in range(flat_ref.shape[0] // 8 * across):
        a, b = at // across, at % across
        low = 8 * (at % per)
        flat_ref[8 * a : 8 * a + 8, 128 * b : 128 * b + 128] = tiles_ref[at // per, low : low + 8, :]
    out_ref[...] = flat_ref[:, 0:channels]
    for copy in copies:
        copy.wait()


def per_device(features, depth_kernel, in_weight, out_weight, decoder_weight, observed, land_mask):
    _, channels, lon_len, lat_len = features.shape
    hid = in_weight.shape[1]
    outputs = decoder_weight.shape[1]
    size = depth_kernel.shape[1]
    half = size // 2
    member_n = lax.axis_size("member")
    space_n = lax.axis_size("space")
    n = member_n * space_n
    members = features.shape[0] * member_n
    total_points = lon_len * space_n * lat_len
    padded_c = round_up(channels, 16)
    pitch = padded_c + 1
    wide_c = round_up(channels, 128)
    tiles = (outputs // 8) * (wide_c // 128)
    per = -(-tiles // n)
    rows = 2 * half
    steps = lon_len // rows
    wide = rows * lat_len
    parts = channels // 128
    grad, summed = pl.pallas_call(
        functools.partial(kernel, (member_n, space_n), half, 1.0 / math.sqrt(members * total_points)),
        name="main",
        out_shape=(
            pltpu.VMEM((channels, lon_len, lat_len), bf16),
            pltpu.VMEM((n, per * 8, 128), f32),
        ),
        in_specs=[ANY_SPEC] * 7,
        out_specs=[VMEM_SPEC, VMEM_SPEC],
        scratch_shapes=[
            pltpu.VMEM((channels, lon_len, lat_len), bf16),
            pltpu.VMEM(((lon_len + 2 * half) * pitch, lat_len), f32),
            pltpu.VMEM((size, size, channels), f32),
            pltpu.VMEM((round_up(size * size, 32), wide_c), f32),
            pltpu.VMEM((wide_c, round_up(size * size, 32)), f32),
            pltpu.VMEM((size * size, padded_c, lat_len), f32),
            pltpu.VMEM((channels, hid), bf16),
            pltpu.VMEM((hid, channels), bf16),
            pltpu.VMEM((channels, hid), bf16),
            pltpu.VMEM((outputs, channels), bf16),
            pltpu.VMEM((channels, outputs), bf16),
            pltpu.VMEM((outputs * lon_len, lat_len), f32),
            pltpu.VMEM((lon_len, lat_len), jnp.int32),
            pltpu.VMEM((rows, padded_c, lat_len), f32),
            pltpu.VMEM((channels, wide), bf16),
            pltpu.VMEM((hid, wide), bf16),
            pltpu.VMEM((steps, channels, wide), bf16),
            pltpu.VMEM((lon_len, outputs, lat_len), bf16),
            pltpu.VMEM((member_n - 1, lon_len, outputs, lat_len), bf16),
            pltpu.VMEM((steps, outputs, wide), bf16),
            pltpu.VMEM((channels, outputs), f32),
            pltpu.VMEM((outputs, wide_c), f32),
            pltpu.VMEM((n, per * 8, 128), bf16),
            pltpu.VMEM((n - 1, per * 8, 128), bf16),
            pltpu.VMEM((per * 8, 128), bf16),
            pltpu.VMEM((n - 1, per * 8, 128), bf16),
            pltpu.VMEM((2, half, padded_c, lat_len), bf16),
            pltpu.VMEM((2, half, padded_c, lat_len), bf16),
            pltpu.SemaphoreType.DMA((6,)),
            pltpu.SemaphoreType.DMA((parts,)),
            pltpu.SemaphoreType.DMA((2, 2)),
            pltpu.SemaphoreType.DMA((2, member_n - 1, steps)),
            pltpu.SemaphoreType.DMA((4, n - 1)),
        ],
        compiler_params=pltpu.CompilerParams(
            collective_id=0, has_side_effects=True, vmem_limit_bytes=54 * 1024 * 1024
        ),
    )(
        features[0], jnp.transpose(depth_kernel, (1, 2, 0)), in_weight, out_weight.T, decoder_weight.T,
        observed.reshape(outputs * lon_len, lat_len), land_mask,
    )
    grad_out, out = pl.pallas_call(
        last_kernel,
        name="last",
        out_shape=(
            jax.ShapeDtypeStruct((channels, lon_len, lat_len), bf16),
            jax.ShapeDtypeStruct((outputs, channels), f32),
        ),
        in_specs=[VMEM_SPEC, VMEM_SPEC],
        out_specs=[ANY_SPEC, VMEM_SPEC],
        scratch_shapes=[
            pltpu.VMEM((outputs, wide_c), f32),
            pltpu.SemaphoreType.DMA((len(spans(channels, 128)),)),
        ],
        compiler_params=pltpu.CompilerParams(vmem_limit_bytes=16 * 1024 * 1024),
    )(grad, summed)
    return (grad_out[None], out.T)


def solution(mesh):
    placed = (
        P("member", None, "space", None),
        P(),
        P(),
        P(),
        P(),
        P(None, "space", None),
        P("space", None),
    )
    return jax.shard_map(
        per_device,
        mesh=mesh,
        in_specs=placed,
        out_specs=(P("member", None, "space", None), P()),
        check_vma=False,
    )
```

```python
import functools
import math

import jax
import jax.numpy as jnp
from jax import lax
from jax.experimental import pallas as pl
from jax.experimental.pallas import tpu as pltpu
from jax.sharding import PartitionSpec as P

norm_eps = 1e-05
MESH = pl.DeviceIdType.MESH
VMEM_SPEC = pl.BlockSpec(memory_space=pltpu.VMEM)
ANY_SPEC = pl.BlockSpec(memory_space=pl.ANY)
f32 = jnp.float32
bf16 = jnp.bfloat16


def round_up(value, step):
    return -(-value // step) * step


def spans(total, width):
    return [(at, min(at + width, total)) for at in range(0, total, width)]


def gelu_of_half(u):
    return u * (1.0 + lax.erf(u * (2.0**0.5)))


def pair_tree(terms):
    while len(terms) > 1:
        terms = [
            terms[i] + terms[i + 1] if i + 1 < len(terms) else terms[i]
            for i in range(0, len(terms), 2)
        ]
    return terms[0]


def interleave(main, side):
    total = sum(share for _, share in main)
    done = 0
    given = 0.0
    for piece, share in main:
        piece()
        given += share
        until = len(side) if given >= total else int(round(len(side) * given / total))
        while done < until:
            side[done]()
            done += 1


def kernel(
    groups, half, scale, x_hbm, taps_hbm, w1_hbm, w2_hbm, dect_hbm, observed_hbm, mask_hbm, grad_ref, out_ref,
    x_ref, plane_ref, taps_in, tin_ref, taps_ref, coef_ref, w1n_ref, w1_ref, w2_ref, dect_ref, dec_ref,
    observed_ref, mask_ref, conv_ref, normed_ref, act_ref, block_ref, own_ref, others_ref, score_ref, tall_ref,
    term_ref, mine, got_member, middle, got_space, piece_ref, quarter, whole, edge_out, edge_in, load_sems, x_sems,
    halo_sems, pair_sems, member_sems, space_sems,
):
    channels, lon_len, lat_len = x_ref.shape
    hid = w1_ref.shape[0]
    size = 2 * half + 1
    pitch = plane_ref.shape[0] // (lon_len + 2 * half)
    rows = 2 * half
    steps = lon_len // rows
    member_n, space_n = groups
    member = lax.axis_index("member")
    space = lax.axis_index("space")
    partners = member_n + space_n - 2

    def other_member(e):
        return lax.rem(member + e + 1, member_n)

    def other_space(e):
        return lax.rem(space + e + 1, space_n)

    barrier = pltpu.get_barrier_semaphore()

    def greet_member(e, carry):
        pl.semaphore_signal(barrier, inc=1, device_id=(other_member(e), space), device_id_type=MESH)
        return carry

    def greet_space(e, carry):
        pl.semaphore_signal(barrier, inc=1, device_id=(member, other_space(e)), device_id_type=MESH)
        return carry

    loads = [
        pltpu.make_async_copy(src, dst, load_sems.at[k])
        for k, (src, dst) in enumerate(
            (
                (w1_hbm, w1n_ref), (taps_hbm, taps_in), (w2_hbm, w2_ref), (dect_hbm, dect_ref),
                (observed_hbm, observed_ref), (mask_hbm, mask_ref),
            )
        )
    ]
    ends = [128 * k for k in range(1, channels // 128)] + [channels]
    parts = list(zip([0] + ends[:-1], ends))
    x_loads = [
        pltpu.make_async_copy(x_hbm.at[low:high], x_ref.at[low:high], x_sems.at[k])
        for k, (low, high) in enumerate(parts)
    ]
    loads[1].start()
    for copy in x_loads:
        copy.start()
    loads[0].start()
    for copy in loads[2:]:
        copy.start()
    lax.fori_loop(0, member_n - 1, greet_member, 0)
    lax.fori_loop(0, space_n - 1, greet_space, 0)

    loads[1].wait()
    tin_ref[...] = jnp.zeros_like(tin_ref)
    for p in range(size):
        tin_ref[size * p : size * (p + 1), 0:channels] = taps_in[p]
    taps_ref[...] = jnp.transpose(tin_ref[...])
    lane = lax.broadcasted_iota(jnp.int32, (16, lat_len), 1)
    inside = []
    for q in range(size):
        shift = half - q
        if shift == 0:
            inside.append(None)
        else:
            ok = lane >= shift if shift > 0 else lane < lat_len + shift
            inside.append(jnp.where(ok, 1.0, 0.0).astype(bf16))

    chunks = -(-channels // 16)

    def spread(first):
        here = pl.ds(first, 16)
        tap = taps_ref[here, :].astype(bf16)
        for at in range(size * size):
            wide = jnp.broadcast_to(tap[:, at : at + 1], (16, lat_len))
            mask = inside[at % size]
            coef_ref[at, here, :] = (wide if mask is None else wide * mask).astype(f32)

    spare = pitch - channels
    for r in range(lon_len + 2 * half):
        plane_ref[r * pitch + channels : (r + 1) * pitch, :] = jnp.zeros((spare, lat_len), f32)

    def turn(c):
        plane_ref[pl.ds(half * pitch + c, lon_len, stride=pitch), :] = x_ref[c].astype(f32)

    def turn16(i, carry):
        spread(pl.multiple_of(i * 16, 16))
        for k in range(16):
            turn(i * 16 + k)
        return carry

    for k, (low, high) in enumerate(parts):
        x_loads[k].wait()
        lax.fori_loop(low // 16, high // 16, turn16, 0)
        if high % 16:
            spread(high // 16 * 16)
        for c in range(high // 16 * 16, high):
            turn(c)
    loads[0].wait()
    for low, high in spans(hid, 256):
        w1_ref[low:high, :] = jnp.transpose(w1n_ref[:, low:high])

    def conv_chunk(first, runs):
        cells = {}
        sums = {}
        for base, count, slot in runs:
            for k in range(count + 2 * half):
                cells[slot, k] = plane_ref[pl.ds((base + k) * pitch + first, 16), :].astype(bf16)
        for q in range(size):
            coef = [coef_ref[p * size + q, pl.ds(first, 16), :].astype(bf16) for p in range(size)]
            for base, count, slot in runs:
                moved = [
                    cells[slot, k] if q == half else pltpu.roll(cells[slot, k], (half - q) % lat_len, 1)
                    for k in range(count + 2 * half)
                ]
                for o in range(count):
                    part = pair_tree([coef[p] * moved[o + p] for p in range(size)])
                    sums.setdefault(slot + o, []).append(part)
        for o, terms in sums.items():
            conv_ref[o, pl.ds(first, 16), :] = pair_tree(terms).astype(f32)

    def conv_pieces(runs):
        return [functools.partial(conv_chunk, 16 * k, runs) for k in range(chunks)]

    def norm_row(r):
        cells = conv_ref[r, 0:channels, :]
        shifted = cells - jnp.sum(cells, axis=0, keepdims=True) * (1.0 / channels)
        square = jnp.sum(shifted * shifted, axis=0, keepdims=True)
        factor = 0.5 * lax.rsqrt(square * (1.0 / channels) + norm_eps)
        normed_ref[:, r * lat_len : (r + 1) * lat_len] = (shifted * factor).astype(bf16)

    def pre_piece():
        pre = jnp.dot(w1_ref[...], normed_ref[...], preferred_element_type=f32)
        act_ref[...] = gelu_of_half(pre).astype(bf16)

    def out_piece(step, lons):
        held = jnp.concatenate([plane_ref[pl.ds((lon + half) * pitch, channels), :] for lon in lons], axis=1)
        out = held + jnp.dot(w2_ref[...], act_ref[...], preferred_element_type=f32)
        block_ref[step] = out.astype(bf16)

    def decode_piece(step):
        decoded = jnp.dot(dect_ref[...], block_ref[step], preferred_element_type=f32).astype(bf16)
        for r in range(rows):
            own_ref[step * rows + r] = decoded[:, r * lat_len : (r + 1) * lat_len]

    def mlp_pieces(step, lons):
        return [
            (pre_piece, 15.0), (functools.partial(out_piece, step, lons), 27.0),
            (functools.partial(decode_piece, step), 1.0),
        ]

    def fused(step, lons, runs):
        norms = [functools.partial(norm_row, r) for r in range(rows)]
        interleave(mlp_pieces(step, lons), conv_pieces(runs) + norms)

    def pair_copy(step, j):
        at = pl.ds(step * rows, rows)
        return pltpu.make_async_remote_copy(
            src_ref=own_ref.at[at], dst_ref=others_ref.at[j, at],
            send_sem=pair_sems.at[0, j, step], recv_sem=pair_sems.at[1, j, step],
            device_id=(lax.rem(member + j + 1, member_n), space), device_id_type=MESH,
        )

    def send_pairs(step):
        for j in range(member_n - 1):
            pair_copy(step, j).start()

    def halo_copy(side):
        to = lax.rem(space + (space_n - 1 if side == 0 else 1), space_n)
        return pltpu.make_async_remote_copy(
            src_ref=edge_out.at[side], dst_ref=edge_in.at[side], send_sem=halo_sems.at[0, side],
            recv_sem=halo_sems.at[1, side], device_id=(member, to), device_id_type=MESH,
        )

    padded = edge_out.shape[2]
    for r in range(half):
        edge_out[0, r] = plane_ref[(half + r) * pitch : (half + r) * pitch + padded, :].astype(bf16)
        edge_out[1, r] = plane_ref[(lon_len + r) * pitch : (lon_len + r) * pitch + padded, :].astype(bf16)

    def conv_loop(k, carry):
        for part in range(2):
            conv_chunk(pl.multiple_of(k * 32 + 16 * part, 16), [(half, rows, 0)])
        return carry

    lax.fori_loop(0, chunks // 2, conv_loop, 0)
    if chunks % 2:
        conv_chunk(16 * chunks - 16, [(half, rows, 0)])
    for r in range(rows):
        norm_row(r)
    pl.semaphore_wait(barrier, partners)
    for side in range(2):
        halo_copy(side).start()
    for copy in loads[2:]:
        copy.wait()
    dec_ref[...] = jnp.transpose(dect_ref[...])

    def lons_of(step):
        return [half + step * rows + r for r in range(rows)]

    def main_loop(step, carry):
        fused(step, lons_of(step), [(half + (step + 1) * rows, rows, 0)])
        send_pairs(step)
        return carry

    lax.fori_loop(0, steps - 2, main_loop, 0)
    for side in range(2):
        halo_copy(side).wait()
    for r in range(half):
        top = (lon_len + half + r) * pitch
        plane_ref[top : top + padded, :] = edge_in[0, r].astype(f32)
        plane_ref[r * pitch : r * pitch + padded, :] = edge_in[1, r].astype(f32)
    fused(steps - 2, lons_of(steps - 2), [(0, half, 0), (lon_len - half, half, half)])
    send_pairs(steps - 2)
    outer = list(range(half)) + list(range(lon_len - half, lon_len))
    tall_ref[...] = jnp.zeros_like(tall_ref)
    term_ref[...] = jnp.zeros_like(term_ref)

    def score_row(step, r, lon):
        at = step * rows + r
        own = own_ref[at].astype(f32)
        misfit = own - observed_ref[pl.ds(lon, own.shape[0], stride=lon_len), :]
        total = misfit * lax.rsqrt(jnp.sum(misfit * misfit, axis=0, keepdims=True) + 1.0)
        pair_sum = jnp.zeros_like(own)
        for k in range(member_n):
            other = own_ref[at] if k == member_n - 1 else others_ref[k, at]
            apart = own - other.astype(f32)
            pair_sum = pair_sum + apart * lax.rsqrt(jnp.sum(apart * apart, axis=0, keepdims=True) + 1.0)
        weight = 4.0 + 8.0 * mask_ref[pl.ds(lon, 1), :].astype(f32)
        score_ref[step, :, r * lat_len : (r + 1) * lat_len] = (
            weight * (total - pair_sum / member_n)
        ).astype(bf16)

    def wait_pairs(step):
        for j in range(member_n - 1):
            pair_copy(step, j).wait()

    def tall_step(step):
        tall_ref[...] += lax.dot_general(
            block_ref[step], score_ref[step], (((1,), (1,)), ((), ())), preferred_element_type=f32
        )

    def score_step(step, lons):
        wait_pairs(step)
        for r in range(rows):
            score_row(step, r, lons[r])
        tall_step(step)

    def grad_step(step, lons):
        grad = jnp.dot(dec_ref[...], score_ref[step], preferred_element_type=f32)
        for r in range(rows):
            plane_ref[pl.ds(lons[r] * pitch, channels), :] = grad[:, r * lat_len : (r + 1) * lat_len]

    def grad_loop(step, carry):
        grad_step(step, lons_of(step))
        return carry

    early = steps - 2
    for step in range(early):
        wait_pairs(step)
    side = []
    for step in range(early):
        side += [functools.partial(score_row, step, r, lons_of(step)[r]) for r in range(rows)]
        side.append(functools.partial(tall_step, step))
    interleave(mlp_pieces(steps - 1, outer), side)
    send_pairs(steps - 1)
    score_step(steps - 2, lons_of(steps - 2))
    lax.fori_loop(0, steps - 1, grad_loop, 0)
    score_step(steps - 1, outer)
    term_ref[:, 0:channels] = scale * jnp.transpose(tall_ref[...])

    share = mine.shape[1] // 8
    tall = term_ref.shape[0] // 8
    across = term_ref.shape[1] // 128
    for at in range(member_n * share):
        low = 8 * (at % share)
        if at < tall * across:
            a, b = at // across, at % across
            tile = term_ref[8 * a : 8 * a + 8, 128 * b : 128 * b + 128].astype(bf16)
        else:
            tile = jnp.zeros((8, 128), bf16)
        mine[at // share, low : low + 8, :] = tile

    def member_copy(kind, e):
        return pltpu.make_async_remote_copy(
            src_ref=mine.at[other_member(e)] if kind == 0 else quarter,
            dst_ref=got_member.at[e] if kind == 0 else whole.at[e],
            send_sem=member_sems.at[kind, 0, e], recv_sem=member_sems.at[kind, 1, e],
            device_id=(other_member(e), space), device_id_type=MESH,
        )

    def space_copy(kind, e):
        return pltpu.make_async_remote_copy(
            src_ref=middle.at[other_space(e)] if kind == 0 else piece_ref,
            dst_ref=got_space.at[e] if kind == 0 else quarter.at[space],
            send_sem=space_sems.at[kind, 0, e], recv_sem=space_sems.at[kind, 1, e],
            device_id=(member, other_space(e)), device_id_type=MESH,
        )

    def start_members(kind):
        for e in range(member_n - 1):
            member_copy(kind, e).start()

    def finish_members(kind):
        for e in range(member_n - 1):
            member_copy(kind, e).wait()

    def start_space(kind):
        def body(e, carry):
            space_copy(kind, e).start()
            return carry

        lax.fori_loop(0, space_n - 1, body, 0)

    def finish_space(kind):
        def body(e, carry):
            space_copy(kind, e).wait()
            return carry

        lax.fori_loop(0, space_n - 1, body, 0)

    def turn_back(c):
        grad_ref[c] = plane_ref[pl.ds(c, lon_len, stride=pitch), :].astype(bf16)

    def turn_back8(i, carry):
        for k in range(8):
            turn_back(i * 8 + k)
        return carry

    def turn_part(k):
        low, high = parts[k]
        lax.fori_loop(low // 8, high // 8, turn_back8, 0)
        for c in range(high // 8 * 8, high):
            turn_back(c)

    start_members(0)
    grad_step(steps - 1, outer)
    first = len(parts) // 2
    for k in range(first):
        turn_part(k)
    finish_members(0)
    high = piece_ref.shape[0]
    total = mine[member].astype(f32)
    for e in range(member_n - 1):
        total = total + got_member[e].astype(f32)
    for k in range(space_n):
        middle[k] = total[k * high : (k + 1) * high, :].astype(bf16)
    start_space(0)
    for k in range(first, len(parts)):
        turn_part(k)
    finish_space(0)
    total = middle[space].astype(f32)
    for e in range(space_n - 1):
        total = total + got_space[e].astype(f32)
    piece_ref[...] = total.astype(bf16)
    start_space(1)
    quarter[space] = piece_ref[...]
    finish_space(1)
    start_members(1)
    out_ref[member] = quarter[...].astype(f32)
    finish_members(1)
    for e in range(member_n - 1):
        out_ref[lax.rem(member + member_n - e - 1, member_n)] = whole[e].astype(f32)


def last_kernel(grad_in, tiles_ref, grad_out, out_ref, flat_ref, sems):
    channels = grad_in.shape[0]
    parts = spans(channels, 128)
    copies = [
        pltpu.make_async_copy(grad_in.at[low:high], grad_out.at[low:high], sems.at[k])
        for k, (low, high) in enumerate(parts)
    ]
    for copy in copies:
        copy.start()
    across = flat_ref.shape[1] // 128
    _, space_n, high, _ = tiles_ref.shape
    per = high // 8
    for at in range(flat_ref.shape[0] // 8 * across):
        a, b = at // across, at % across
        low = 8 * (at % per)
        flat_ref[8 * a : 8 * a + 8, 128 * b : 128 * b + 128] = tiles_ref[
            at // (per * space_n), at // per % space_n, low : low + 8, :
        ]
    out_ref[...] = flat_ref[:, 0:channels]
    for copy in copies:
        copy.wait()


def per_device(features, depth_kernel, in_weight, out_weight, decoder_weight, observed, land_mask):
    _, channels, lon_len, lat_len = features.shape
    hid = in_weight.shape[1]
    outputs = decoder_weight.shape[1]
    size = depth_kernel.shape[1]
    half = size // 2
    member_n = lax.axis_size("member")
    space_n = lax.axis_size("space")
    n = member_n * space_n
    members = features.shape[0] * member_n
    total_points = lon_len * space_n * lat_len
    padded_c = round_up(channels, 16)
    pitch = padded_c + 1
    wide_c = round_up(channels, 128)
    tiles = (outputs // 8) * (wide_c // 128)
    per = 2 * -(-tiles // (2 * n))
    rows = 2 * half
    steps = lon_len // rows
    wide = rows * lat_len
    parts = channels // 128
    grad, summed = pl.pallas_call(
        functools.partial(kernel, (member_n, space_n), half, 1.0 / math.sqrt(members * total_points)),
        name="main",
        out_shape=(
            pltpu.VMEM((channels, lon_len, lat_len), bf16),
            pltpu.VMEM((member_n, space_n, per * 8, 128), f32),
        ),
        in_specs=[ANY_SPEC] * 7,
        out_specs=[VMEM_SPEC, VMEM_SPEC],
        scratch_shapes=[
            pltpu.VMEM((channels, lon_len, lat_len), bf16),
            pltpu.VMEM(((lon_len + 2 * half) * pitch, lat_len), f32),
            pltpu.VMEM((size, size, channels), f32),
            pltpu.VMEM((round_up(size * size, 32), wide_c), f32),
            pltpu.VMEM((wide_c, round_up(size * size, 32)), f32),
            pltpu.VMEM((size * size, padded_c, lat_len), f32),
            pltpu.VMEM((channels, hid), bf16),
            pltpu.VMEM((hid, channels), bf16),
            pltpu.VMEM((channels, hid), bf16),
            pltpu.VMEM((outputs, channels), bf16),
            pltpu.VMEM((channels, outputs), bf16),
            pltpu.VMEM((outputs * lon_len, lat_len), f32),
            pltpu.VMEM((lon_len, lat_len), jnp.int32),
            pltpu.VMEM((rows, padded_c, lat_len), f32),
            pltpu.VMEM((channels, wide), bf16),
            pltpu.VMEM((hid, wide), bf16),
            pltpu.VMEM((steps, channels, wide), bf16),
            pltpu.VMEM((lon_len, outputs, lat_len), bf16),
            pltpu.VMEM((member_n - 1, lon_len, outputs, lat_len), bf16),
            pltpu.VMEM((steps, outputs, wide), bf16),
            pltpu.VMEM((channels, outputs), f32),
            pltpu.VMEM((outputs, wide_c), f32),
            pltpu.VMEM((member_n, space_n * per * 8, 128), bf16),
            pltpu.VMEM((member_n - 1, space_n * per * 8, 128), bf16),
            pltpu.VMEM((space_n, per * 8, 128), bf16),
            pltpu.VMEM((space_n - 1, per * 8, 128), bf16),
            pltpu.VMEM((per * 8, 128), bf16),
            pltpu.VMEM((space_n, per * 8, 128), bf16),
            pltpu.VMEM((member_n - 1, space_n, per * 8, 128), bf16),
            pltpu.VMEM((2, half, padded_c, lat_len), bf16),
            pltpu.VMEM((2, half, padded_c, lat_len), bf16),
            pltpu.SemaphoreType.DMA((6,)),
            pltpu.SemaphoreType.DMA((parts,)),
            pltpu.SemaphoreType.DMA((2, 2)),
            pltpu.SemaphoreType.DMA((2, member_n - 1, steps)),
            pltpu.SemaphoreType.DMA((2, 2, member_n - 1)),
            pltpu.SemaphoreType.DMA((2, 2, space_n - 1)),
        ],
        compiler_params=pltpu.CompilerParams(
            collective_id=0, has_side_effects=True, vmem_limit_bytes=54 * 1024 * 1024
        ),
    )(
        features[0], jnp.transpose(depth_kernel, (1, 2, 0)), in_weight, out_weight.T, decoder_weight.T,
        observed.reshape(outputs * lon_len, lat_len), land_mask,
    )
    grad_out, out = pl.pallas_call(
        last_kernel,
        name="last",
        out_shape=(
            jax.ShapeDtypeStruct((channels, lon_len, lat_len), bf16),
            jax.ShapeDtypeStruct((outputs, channels), f32),
        ),
        in_specs=[VMEM_SPEC, VMEM_SPEC],
        out_specs=[ANY_SPEC, VMEM_SPEC],
        scratch_shapes=[
            pltpu.VMEM((outputs, wide_c), f32),
            pltpu.SemaphoreType.DMA((len(spans(channels, 128)),)),
        ],
        compiler_params=pltpu.CompilerParams(vmem_limit_bytes=16 * 1024 * 1024),
    )(grad, summed)
    return (grad_out[None], out.T)


def solution(mesh):
    placed = (
        P("member", None, "space", None),
        P(),
        P(),
        P(),
        P(),
        P(None, "space", None),
        P("space", None),
    )
    return jax.shard_map(
        per_device,
        mesh=mesh,
        in_specs=placed,
        out_specs=(P("member", None, "space", None), P()),
        check_vma=False,
    )
```

```python
import functools
import math

import jax
import jax.numpy as jnp
from jax import lax
from jax.experimental import pallas as pl
from jax.experimental.pallas import tpu as pltpu
from jax.sharding import PartitionSpec as P

norm_eps = 1e-05
MESH = pl.DeviceIdType.MESH
VMEM_SPEC = pl.BlockSpec(memory_space=pltpu.VMEM)
ANY_SPEC = pl.BlockSpec(memory_space=pl.ANY)
f32 = jnp.float32
bf16 = jnp.bfloat16


def round_up(value, step):
    return -(-value // step) * step


def spans(total, width):
    return [(at, min(at + width, total)) for at in range(0, total, width)]


def gelu_of_half(u):
    return u * (1.0 + lax.erf(u * (2.0**0.5)))


def pair_tree(terms):
    while len(terms) > 1:
        terms = [
            terms[i] + terms[i + 1] if i + 1 < len(terms) else terms[i]
            for i in range(0, len(terms), 2)
        ]
    return terms[0]


def interleave(main, side):
    total = sum(share for _, share in main)
    done = 0
    given = 0.0
    for piece, share in main:
        piece()
        given += share
        until = len(side) if given >= total else int(round(len(side) * given / total))
        while done < until:
            side[done]()
            done += 1


def kernel(
    groups, half, scale, x_hbm, taps_hbm, w1_hbm, w2_hbm, dect_hbm, observed_hbm, mask_hbm, grad_ref, out_ref,
    x_ref, plane_ref, taps_in, tin_ref, taps_ref, coef_ref, w1n_ref, w1_ref, w2_ref, dect_ref, dec_ref,
    observed_ref, mask_ref, conv_ref, normed_ref, act_ref, block_ref, own_ref, others_ref, score_ref, tall_ref,
    term_ref, mine, got, mine_sum, whole, edge_out, edge_in, load_sems, x_sems, halo_sems, pair_sems, sems,
):
    channels, lon_len, lat_len = x_ref.shape
    hid = w1_ref.shape[0]
    size = 2 * half + 1
    pitch = plane_ref.shape[0] // (lon_len + 2 * half)
    rows = 2 * half
    steps = lon_len // rows
    member_n, space_n = groups
    member = lax.axis_index("member")
    space = lax.axis_index("space")
    n = member_n * space_n
    me = member * space_n + space

    def peer(e):
        other = lax.rem(me + e + 1, n)
        return other, (other // space_n, lax.rem(other, space_n))

    barrier = pltpu.get_barrier_semaphore()

    def greet(e, carry):
        pl.semaphore_signal(barrier, inc=1, device_id=peer(e)[1], device_id_type=MESH)
        return carry

    loads = [
        pltpu.make_async_copy(src, dst, load_sems.at[k])
        for k, (src, dst) in enumerate(
            (
                (w1_hbm, w1n_ref), (taps_hbm, taps_in), (w2_hbm, w2_ref), (dect_hbm, dect_ref),
                (observed_hbm, observed_ref), (mask_hbm, mask_ref),
            )
        )
    ]
    ends = [128 * k for k in range(1, channels // 128)] + [channels]
    parts = list(zip([0] + ends[:-1], ends))
    x_loads = [
        pltpu.make_async_copy(x_hbm.at[low:high], x_ref.at[low:high], x_sems.at[k])
        for k, (low, high) in enumerate(parts)
    ]
    loads[1].start()
    for copy in x_loads:
        copy.start()
    loads[0].start()
    for copy in loads[2:]:
        copy.start()
    lax.fori_loop(0, n - 1, greet, 0)

    loads[1].wait()
    tin_ref[...] = jnp.zeros_like(tin_ref)
    for p in range(size):
        tin_ref[size * p : size * (p + 1), 0:channels] = taps_in[p]
    taps_ref[...] = jnp.transpose(tin_ref[...])
    lane = lax.broadcasted_iota(jnp.int32, (16, lat_len), 1)
    inside = []
    for q in range(size):
        shift = half - q
        if shift == 0:
            inside.append(None)
        else:
            ok = lane >= shift if shift > 0 else lane < lat_len + shift
            inside.append(jnp.where(ok, 1.0, 0.0).astype(bf16))

    chunks = -(-channels // 16)

    def spread(first):
        here = pl.ds(first, 16)
        tap = taps_ref[here, :].astype(bf16)

        def one(p, q):
            at = p * size + q
            wide = jnp.broadcast_to(tap[:, at : at + 1], (16, lat_len))
            wide = wide if inside[q] is None else wide * inside[q]
            coef_ref[at, here, :] = wide.astype(f32)
            return wide

        return one

    def kept(first):
        here = pl.ds(first, 16)
        return lambda p, q: coef_ref[p * size + q, here, :].astype(bf16)

    spare = pitch - channels
    for r in range(lon_len + 2 * half):
        plane_ref[r * pitch + channels : (r + 1) * pitch, :] = jnp.zeros((spare, lat_len), f32)

    def turn(c):
        plane_ref[pl.ds(half * pitch + c, lon_len, stride=pitch), :] = x_ref[c].astype(f32)

    def conv_chunk(first, runs, source=kept):
        coef_of = source(first)
        cells = {}
        sums = {}
        for base, count, slot in runs:
            for k in range(count + 2 * half):
                cells[slot, k] = plane_ref[pl.ds((base + k) * pitch + first, 16), :].astype(bf16)
        for q in range(size):
            coef = [coef_of(p, q) for p in range(size)]
            for base, count, slot in runs:
                moved = [
                    cells[slot, k] if q == half else pltpu.roll(cells[slot, k], (half - q) % lat_len, 1)
                    for k in range(count + 2 * half)
                ]
                for o in range(count):
                    part = pair_tree([coef[p] * moved[o + p] for p in range(size)])
                    sums.setdefault(slot + o, []).append(part)
        for o, terms in sums.items():
            conv_ref[o, pl.ds(first, 16), :] = pair_tree(terms).astype(f32)

    inner = [(half, rows, 0)]

    def turn16(i):
        for k in range(16):
            turn(i * 16 + k)

    def head(i, carry):
        for part in range(2):
            conv_chunk(pl.multiple_of(i * 32 + 16 * (part - 2), 16), inner, spread)
        for part in range(2):
            turn16(i * 2 + part)
        return carry

    for k, (low, high) in enumerate(parts):
        x_loads[k].wait()
        if k == 0:
            turn16(0)
            turn16(1)
        lax.fori_loop(max(low // 32, 1), high // 32, head, 0)
    for c in range(channels // 32 * 32, channels):
        turn(c)
    for at in range(channels // 32 * 2 - 2, chunks):
        conv_chunk(16 * at, inner, spread)
    loads[0].wait()
    for low, high in spans(hid, 256):
        w1_ref[low:high, :] = jnp.transpose(w1n_ref[:, low:high])

    def conv_pieces(runs):
        return [functools.partial(conv_chunk, 16 * k, runs) for k in range(chunks)]

    def norm_row(r):
        cells = conv_ref[r, 0:channels, :]
        shifted = cells - jnp.sum(cells, axis=0, keepdims=True) * (1.0 / channels)
        square = jnp.sum(shifted * shifted, axis=0, keepdims=True)
        factor = 0.5 * lax.rsqrt(square * (1.0 / channels) + norm_eps)
        normed_ref[:, r * lat_len : (r + 1) * lat_len] = (shifted * factor).astype(bf16)

    def pre_piece():
        pre = jnp.dot(w1_ref[...], normed_ref[...], preferred_element_type=f32)
        act_ref[...] = gelu_of_half(pre).astype(bf16)

    def out_piece(step, lons):
        held = jnp.concatenate([plane_ref[pl.ds((lon + half) * pitch, channels), :] for lon in lons], axis=1)
        out = held + jnp.dot(w2_ref[...], act_ref[...], preferred_element_type=f32)
        block_ref[step] = out.astype(bf16)

    def decode_piece(step):
        decoded = jnp.dot(dect_ref[...], block_ref[step], preferred_element_type=f32).astype(bf16)
        for r in range(rows):
            own_ref[step * rows + r] = decoded[:, r * lat_len : (r + 1) * lat_len]

    def mlp_pieces(step, lons):
        return [
            (pre_piece, 15.0), (functools.partial(out_piece, step, lons), 27.0),
            (functools.partial(decode_piece, step), 1.0),
        ]

    def fused(step, lons, runs):
        norms = [functools.partial(norm_row, r) for r in range(rows)]
        interleave(mlp_pieces(step, lons), conv_pieces(runs) + norms)

    def pair_copy(step, j):
        at = pl.ds(step * rows, rows)
        return pltpu.make_async_remote_copy(
            src_ref=own_ref.at[at], dst_ref=others_ref.at[j, at],
            send_sem=pair_sems.at[0, j, step], recv_sem=pair_sems.at[1, j, step],
            device_id=(lax.rem(member + j + 1, member_n), space), device_id_type=MESH,
        )

    def send_pairs(step):
        for j in range(member_n - 1):
            pair_copy(step, j).start()

    def halo_copy(side):
        to = lax.rem(space + (space_n - 1 if side == 0 else 1), space_n)
        return pltpu.make_async_remote_copy(
            src_ref=edge_out.at[side], dst_ref=edge_in.at[side], send_sem=halo_sems.at[0, side],
            recv_sem=halo_sems.at[1, side], device_id=(member, to), device_id_type=MESH,
        )

    padded = edge_out.shape[2]
    for r in range(half):
        edge_out[0, r] = plane_ref[(half + r) * pitch : (half + r) * pitch + padded, :].astype(bf16)
        edge_out[1, r] = plane_ref[(lon_len + r) * pitch : (lon_len + r) * pitch + padded, :].astype(bf16)

    for r in range(rows):
        norm_row(r)
    pl.semaphore_wait(barrier, n - 1)
    for side in range(2):
        halo_copy(side).start()
    for copy in loads[2:]:
        copy.wait()
    dec_ref[...] = jnp.transpose(dect_ref[...])

    def lons_of(step):
        return [half + step * rows + r for r in range(rows)]

    def main_loop(step, carry):
        fused(step, lons_of(step), [(half + (step + 1) * rows, rows, 0)])
        send_pairs(step)
        return carry

    lax.fori_loop(0, steps - 2, main_loop, 0)
    for side in range(2):
        halo_copy(side).wait()
    for r in range(half):
        top = (lon_len + half + r) * pitch
        plane_ref[top : top + padded, :] = edge_in[0, r].astype(f32)
        plane_ref[r * pitch : r * pitch + padded, :] = edge_in[1, r].astype(f32)
    fused(steps - 2, lons_of(steps - 2), [(0, half, 0), (lon_len - half, half, half)])
    send_pairs(steps - 2)
    outer = list(range(half)) + list(range(lon_len - half, lon_len))
    tall_ref[...] = jnp.zeros_like(tall_ref)
    term_ref[...] = jnp.zeros_like(term_ref)

    def score_row(step, r, lon):
        at = step * rows + r
        own = own_ref[at].astype(f32)
        misfit = own - observed_ref[pl.ds(lon, own.shape[0], stride=lon_len), :]
        total = misfit * lax.rsqrt(jnp.sum(misfit * misfit, axis=0, keepdims=True) + 1.0)
        pair_sum = jnp.zeros_like(own)
        for k in range(member_n):
            other = own_ref[at] if k == member_n - 1 else others_ref[k, at]
            apart = own - other.astype(f32)
            pair_sum = pair_sum + apart * lax.rsqrt(jnp.sum(apart * apart, axis=0, keepdims=True) + 1.0)
        weight = 4.0 + 8.0 * mask_ref[pl.ds(lon, 1), :].astype(f32)
        score_ref[step, :, r * lat_len : (r + 1) * lat_len] = (
            weight * (total - pair_sum / member_n)
        ).astype(bf16)

    def wait_pairs(step):
        for j in range(member_n - 1):
            pair_copy(step, j).wait()

    def tall_step(step):
        tall_ref[...] += lax.dot_general(
            block_ref[step], score_ref[step], (((1,), (1,)), ((), ())), preferred_element_type=f32
        )

    def score_step(step, lons):
        wait_pairs(step)
        for r in range(rows):
            score_row(step, r, lons[r])
        tall_step(step)

    def grad_step(step, lons):
        grad = jnp.dot(dec_ref[...], score_ref[step], preferred_element_type=f32)
        for r in range(rows):
            plane_ref[pl.ds(lons[r] * pitch, channels), :] = grad[:, r * lat_len : (r + 1) * lat_len]

    def grad_loop(step, carry):
        grad_step(step, lons_of(step))
        return carry

    early = steps - 3
    for step in range(early):
        wait_pairs(step)
    side = []
    for step in range(early):
        side += [functools.partial(score_row, step, r, lons_of(step)[r]) for r in range(rows)]
        side.append(functools.partial(tall_step, step))
    interleave(mlp_pieces(steps - 1, outer), side)
    send_pairs(steps - 1)
    for step in range(early, steps - 1):
        score_step(step, lons_of(step))
    lax.fori_loop(0, steps - 1, grad_loop, 0)
    score_step(steps - 1, outer)
    term_ref[:, 0:channels] = scale * jnp.transpose(tall_ref[...])

    per = mine_sum.shape[0] // 8
    tall = term_ref.shape[0] // 8
    across = term_ref.shape[1] // 128
    for at in range(n * per):
        low = 8 * (at % per)
        if at < tall * across:
            a, b = at // across, at % across
            tile = term_ref[8 * a : 8 * a + 8, 128 * b : 128 * b + 128].astype(bf16)
        else:
            tile = jnp.zeros((8, 128), bf16)
        mine[at // per, low : low + 8, :] = tile

    def scatter_copy(e):
        other, device = peer(e)
        return pltpu.make_async_remote_copy(
            src_ref=mine.at[other], dst_ref=got.at[e], send_sem=sems.at[0, e],
            recv_sem=sems.at[1, e], device_id=device, device_id_type=MESH,
        )

    def gather_copy(e):
        _, device = peer(e)
        return pltpu.make_async_remote_copy(
            src_ref=mine_sum, dst_ref=whole.at[e], send_sem=sems.at[2, e],
            recv_sem=sems.at[3, e], device_id=device, device_id_type=MESH,
        )

    def each(act, unroll):
        def body(e, carry):
            act(e)
            return carry

        lax.fori_loop(0, n - 1, body, 0, unroll=unroll)

    def start(make):
        each(lambda e: make(e).start(), 1)

    def finish(make):
        each(lambda e: make(e).wait(), 1)

    def turn_back(c):
        grad_ref[c] = plane_ref[pl.ds(c, lon_len, stride=pitch), :].astype(bf16)

    def turn_back8(i, carry):
        for k in range(8):
            turn_back(i * 8 + k)
        return carry

    def turn_part(k):
        low, high = parts[k]
        lax.fori_loop(low // 8, high // 8, turn_back8, 0)
        for c in range(high // 8 * 8, high):
            turn_back(c)

    start(scatter_copy)
    grad_step(steps - 1, outer)
    first = len(parts) - 1
    for k in range(first):
        turn_part(k)
    finish(scatter_copy)
    total = mine[me].astype(f32)
    for e in range(n - 1):
        total = total + got[e].astype(f32)
    mine_sum[...] = total.astype(bf16)
    start(gather_copy)
    out_ref[me] = mine_sum[...].astype(f32)
    for k in range(first, len(parts)):
        turn_part(k)
    finish(gather_copy)
    for e in range(n - 1):
        out_ref[lax.rem(me + n - e - 1, n)] = whole[e].astype(f32)


def last_kernel(grad_in, tiles_ref, grad_out, out_ref, flat_ref, sems):
    channels = grad_in.shape[0]
    parts = spans(channels, 128)
    copies = [
        pltpu.make_async_copy(grad_in.at[low:high], grad_out.at[low:high], sems.at[k])
        for k, (low, high) in enumerate(parts)
    ]
    for copy in copies:
        copy.start()
    across = flat_ref.shape[1] // 128
    per = tiles_ref.shape[1] // 8
    for at in range(flat_ref.shape[0] // 8 * across):
        a, b = at // across, at % across
        low = 8 * (at % per)
        flat_ref[8 * a : 8 * a + 8, 128 * b : 128 * b + 128] = tiles_ref[at // per, low : low + 8, :]
    out_ref[...] = flat_ref[:, 0:channels]
    for copy in copies:
        copy.wait()


def per_device(features, depth_kernel, in_weight, out_weight, decoder_weight, observed, land_mask):
    _, channels, lon_len, lat_len = features.shape
    hid = in_weight.shape[1]
    outputs = decoder_weight.shape[1]
    size = depth_kernel.shape[1]
    half = size // 2
    member_n = lax.axis_size("member")
    space_n = lax.axis_size("space")
    n = member_n * space_n
    members = features.shape[0] * member_n
    total_points = lon_len * space_n * lat_len
    padded_c = round_up(channels, 16)
    pitch = padded_c + 1
    wide_c = round_up(channels, 128)
    tiles = (outputs // 8) * (wide_c // 128)
    per = -(-tiles // n)
    rows = 2 * half
    steps = lon_len // rows
    wide = rows * lat_len
    parts = channels // 128
    grad, summed = pl.pallas_call(
        functools.partial(kernel, (member_n, space_n), half, 1.0 / math.sqrt(members * total_points)),
        name="main",
        out_shape=(
            pltpu.VMEM((channels, lon_len, lat_len), bf16),
            pltpu.VMEM((n, per * 8, 128), f32),
        ),
        in_specs=[ANY_SPEC] * 7,
        out_specs=[VMEM_SPEC, VMEM_SPEC],
        scratch_shapes=[
            pltpu.VMEM((channels, lon_len, lat_len), bf16),
            pltpu.VMEM(((lon_len + 2 * half) * pitch, lat_len), f32),
            pltpu.VMEM((size, size, channels), f32),
            pltpu.VMEM((round_up(size * size, 32), wide_c), f32),
            pltpu.VMEM((wide_c, round_up(size * size, 32)), f32),
            pltpu.VMEM((size * size, padded_c, lat_len), f32),
            pltpu.VMEM((channels, hid), bf16),
            pltpu.VMEM((hid, channels), bf16),
            pltpu.VMEM((channels, hid), bf16),
            pltpu.VMEM((outputs, channels), bf16),
            pltpu.VMEM((channels, outputs), bf16),
            pltpu.VMEM((outputs * lon_len, lat_len), f32),
            pltpu.VMEM((lon_len, lat_len), jnp.int32),
            pltpu.VMEM((rows, padded_c, lat_len), f32),
            pltpu.VMEM((channels, wide), bf16),
            pltpu.VMEM((hid, wide), bf16),
            pltpu.VMEM((steps, channels, wide), bf16),
            pltpu.VMEM((lon_len, outputs, lat_len), bf16),
            pltpu.VMEM((member_n - 1, lon_len, outputs, lat_len), bf16),
            pltpu.VMEM((steps, outputs, wide), bf16),
            pltpu.VMEM((channels, outputs), f32),
            pltpu.VMEM((outputs, wide_c), f32),
            pltpu.VMEM((n, per * 8, 128), bf16),
            pltpu.VMEM((n - 1, per * 8, 128), bf16),
            pltpu.VMEM((per * 8, 128), bf16),
            pltpu.VMEM((n - 1, per * 8, 128), bf16),
            pltpu.VMEM((2, half, padded_c, lat_len), bf16),
            pltpu.VMEM((2, half, padded_c, lat_len), bf16),
            pltpu.SemaphoreType.DMA((6,)),
            pltpu.SemaphoreType.DMA((parts,)),
            pltpu.SemaphoreType.DMA((2, 2)),
            pltpu.SemaphoreType.DMA((2, member_n - 1, steps)),
            pltpu.SemaphoreType.DMA((4, n - 1)),
        ],
        compiler_params=pltpu.CompilerParams(
            collective_id=0, has_side_effects=True, vmem_limit_bytes=54 * 1024 * 1024
        ),
    )(
        features[0], jnp.transpose(depth_kernel, (1, 2, 0)), in_weight, out_weight.T, decoder_weight.T,
        observed.reshape(outputs * lon_len, lat_len), land_mask,
    )
    grad_out, out = pl.pallas_call(
        last_kernel,
        name="last",
        out_shape=(
            jax.ShapeDtypeStruct((channels, lon_len, lat_len), bf16),
            jax.ShapeDtypeStruct((outputs, channels), f32),
        ),
        in_specs=[VMEM_SPEC, VMEM_SPEC],
        out_specs=[ANY_SPEC, VMEM_SPEC],
        scratch_shapes=[
            pltpu.VMEM((outputs, wide_c), f32),
            pltpu.SemaphoreType.DMA((len(spans(channels, 128)),)),
        ],
        compiler_params=pltpu.CompilerParams(vmem_limit_bytes=16 * 1024 * 1024),
    )(grad, summed)
    return (grad_out[None], out.T)


def solution(mesh):
    placed = (
        P("member", None, "space", None),
        P(),
        P(),
        P(),
        P(),
        P(None, "space", None),
        P("space", None),
    )
    return jax.shard_map(
        per_device,
        mesh=mesh,
        in_specs=placed,
        out_specs=(P("member", None, "space", None), P()),
        check_vma=False,
    )
```

```python
import functools
import math

import jax
import jax.numpy as jnp
from jax import lax
from jax.experimental import pallas as pl
from jax.experimental.pallas import tpu as pltpu
from jax.sharding import PartitionSpec as P

norm_eps = 1e-05
MESH = pl.DeviceIdType.MESH
VMEM_SPEC = pl.BlockSpec(memory_space=pltpu.VMEM)
ANY_SPEC = pl.BlockSpec(memory_space=pl.ANY)
f32 = jnp.float32
bf16 = jnp.bfloat16


def round_up(value, step):
    return -(-value // step) * step


def spans(total, width):
    return [(at, min(at + width, total)) for at in range(0, total, width)]


def gelu_of_half(u):
    return u * (1.0 + lax.erf(u * (2.0**0.5)))


def pair_tree(terms):
    while len(terms) > 1:
        terms = [
            terms[i] + terms[i + 1] if i + 1 < len(terms) else terms[i]
            for i in range(0, len(terms), 2)
        ]
    return terms[0]


def interleave(main, side):
    total = sum(share for _, share in main)
    done = 0
    given = 0.0
    for piece, share in main:
        piece()
        given += share
        until = len(side) if given >= total else int(round(len(side) * given / total))
        while done < until:
            side[done]()
            done += 1


def kernel(
    groups, half, scale, x_hbm, taps_hbm, w1_hbm, w2_hbm, dect_hbm, observed_hbm, mask_hbm, grad_ref, out_ref,
    x_ref, plane_ref, taps_in, tin_ref, taps_ref, coef_ref, w1n_ref, w1_ref, w2_ref, dect_ref, dec_ref,
    observed_ref, mask_ref, conv_ref, normed_ref, act_ref, block_ref, own_ref, others_ref, score_ref, tall_ref,
    term_ref, mine, got, mine_sum, whole, edge_out, edge_in, load_sems, x_sems, halo_sems, pair_sems, sems,
):
    channels, lon_len, lat_len = x_ref.shape
    hid = w1_ref.shape[0]
    size = 2 * half + 1
    pitch = plane_ref.shape[0] // (lon_len + 2 * half)
    rows = 2 * half
    steps = lon_len // rows
    member_n, space_n = groups
    member = lax.axis_index("member")
    space = lax.axis_index("space")
    n = member_n * space_n
    me = member * space_n + space

    def peer(e):
        other = lax.rem(me + e + 1, n)
        return other, (other // space_n, lax.rem(other, space_n))

    barrier = pltpu.get_barrier_semaphore()

    def greet(e, carry):
        pl.semaphore_signal(barrier, inc=1, device_id=peer(e)[1], device_id_type=MESH)
        return carry

    loads = [
        pltpu.make_async_copy(src, dst, load_sems.at[k])
        for k, (src, dst) in enumerate(
            (
                (w1_hbm, w1n_ref), (taps_hbm, taps_in), (w2_hbm, w2_ref), (dect_hbm, dect_ref),
                (observed_hbm, observed_ref), (mask_hbm, mask_ref),
            )
        )
    ]
    ends = [128 * k for k in range(1, channels // 128)] + [channels]
    parts = list(zip([0] + ends[:-1], ends))
    x_loads = [
        pltpu.make_async_copy(x_hbm.at[low:high], x_ref.at[low:high], x_sems.at[k])
        for k, (low, high) in enumerate(parts)
    ]
    loads[1].start()
    for copy in x_loads:
        copy.start()
    loads[0].start()
    for copy in loads[2:]:
        copy.start()
    lax.fori_loop(0, n - 1, greet, 0)

    loads[1].wait()
    tin_ref[...] = jnp.zeros_like(tin_ref)
    for p in range(size):
        tin_ref[size * p : size * (p + 1), 0:channels] = taps_in[p]
    taps_ref[...] = jnp.transpose(tin_ref[...])
    lane = lax.broadcasted_iota(jnp.int32, (16, lat_len), 1)
    inside = []
    for q in range(size):
        shift = half - q
        if shift == 0:
            inside.append(None)
        else:
            ok = lane >= shift if shift > 0 else lane < lat_len + shift
            inside.append(jnp.where(ok, 1.0, 0.0).astype(bf16))

    chunks = -(-channels // 16)

    def spread(first):
        here = pl.ds(first, 16)
        tap = taps_ref[here, :].astype(bf16)

        def one(p, q):
            at = p * size + q
            wide = jnp.broadcast_to(tap[:, at : at + 1], (16, lat_len))
            wide = wide if inside[q] is None else wide * inside[q]
            coef_ref[at, here, :] = wide.astype(f32)
            return wide

        return one

    def kept(first):
        here = pl.ds(first, 16)
        return lambda p, q: coef_ref[p * size + q, here, :].astype(bf16)

    spare = pitch - channels
    for r in range(lon_len + 2 * half):
        plane_ref[r * pitch + channels : (r + 1) * pitch, :] = jnp.zeros((spare, lat_len), f32)

    def turn(c):
        plane_ref[pl.ds(half * pitch + c, lon_len, stride=pitch), :] = x_ref[c].astype(f32)

    def conv_chunk(first, runs, source=kept):
        coef_of = source(first)
        cells = {}
        sums = {}
        for base, count, slot in runs:
            for k in range(count + 2 * half):
                cells[slot, k] = plane_ref[pl.ds((base + k) * pitch + first, 16), :].astype(bf16)
        for q in range(size):
            coef = [coef_of(p, q) for p in range(size)]
            for base, count, slot in runs:
                moved = [
                    cells[slot, k] if q == half else pltpu.roll(cells[slot, k], (half - q) % lat_len, 1)
                    for k in range(count + 2 * half)
                ]
                for o in range(count):
                    part = pair_tree([coef[p] * moved[o + p] for p in range(size)])
                    sums.setdefault(slot + o, []).append(part)
        for o, terms in sums.items():
            conv_ref[o, pl.ds(first, 16), :] = pair_tree(terms).astype(f32)

    inner = [(half, rows, 0)]

    def turn16(i):
        for k in range(16):
            turn(i * 16 + k)

    def head(i, carry):
        for part in range(2):
            conv_chunk(pl.multiple_of(i * 32 + 16 * (part - 2), 16), inner, spread)
        for part in range(2):
            turn16(i * 2 + part)
        return carry

    for k, (low, high) in enumerate(parts):
        x_loads[k].wait()
        if k == 0:
            turn16(0)
            turn16(1)
        lax.fori_loop(max(low // 32, 1), high // 32, head, 0)
    for c in range(channels // 32 * 32, channels):
        turn(c)
    for at in range(channels // 32 * 2 - 2, chunks):
        conv_chunk(16 * at, inner, spread)
    loads[0].wait()
    for low, high in spans(hid, 256):
        w1_ref[low:high, :] = jnp.transpose(w1n_ref[:, low:high])

    def conv_pieces(runs):
        return [functools.partial(conv_chunk, 16 * k, runs) for k in range(chunks)]

    def norm_row(r):
        cells = conv_ref[r, 0:channels, :]
        shifted = cells - jnp.sum(cells, axis=0, keepdims=True) * (1.0 / channels)
        square = jnp.sum(shifted * shifted, axis=0, keepdims=True)
        factor = 0.5 * lax.rsqrt(square * (1.0 / channels) + norm_eps)
        normed_ref[:, r * lat_len : (r + 1) * lat_len] = (shifted * factor).astype(bf16)

    def pre_piece():
        pre = jnp.dot(w1_ref[...], normed_ref[...], preferred_element_type=f32)
        act_ref[...] = gelu_of_half(pre).astype(bf16)

    def out_piece(step, lons):
        held = jnp.concatenate([plane_ref[pl.ds((lon + half) * pitch, channels), :] for lon in lons], axis=1)
        out = held + jnp.dot(w2_ref[...], act_ref[...], preferred_element_type=f32)
        block_ref[step] = out.astype(bf16)

    def decode_piece(step):
        decoded = jnp.dot(dect_ref[...], block_ref[step], preferred_element_type=f32).astype(bf16)
        for r in range(rows):
            own_ref[step * rows + r] = decoded[:, r * lat_len : (r + 1) * lat_len]

    def mlp_pieces(step, lons):
        return [
            (pre_piece, 15.0), (functools.partial(out_piece, step, lons), 27.0),
            (functools.partial(decode_piece, step), 1.0),
        ]

    def fused(step, lons, runs):
        norms = [functools.partial(norm_row, r) for r in range(rows)]
        interleave(mlp_pieces(step, lons), conv_pieces(runs) + norms)

    def pair_copy(step, j):
        at = pl.ds(step * rows, rows)
        return pltpu.make_async_remote_copy(
            src_ref=own_ref.at[at], dst_ref=others_ref.at[j, at],
            send_sem=pair_sems.at[0, j, step], recv_sem=pair_sems.at[1, j, step],
            device_id=(lax.rem(member + j + 1, member_n), space), device_id_type=MESH,
        )

    def send_pairs(step):
        for j in range(member_n - 1):
            pair_copy(step, j).start()

    def halo_copy(side):
        to = lax.rem(space + (space_n - 1 if side == 0 else 1), space_n)
        return pltpu.make_async_remote_copy(
            src_ref=edge_out.at[side], dst_ref=edge_in.at[side], send_sem=halo_sems.at[0, side],
            recv_sem=halo_sems.at[1, side], device_id=(member, to), device_id_type=MESH,
        )

    padded = edge_out.shape[2]
    for r in range(half):
        edge_out[0, r] = plane_ref[(half + r) * pitch : (half + r) * pitch + padded, :].astype(bf16)
        edge_out[1, r] = plane_ref[(lon_len + r) * pitch : (lon_len + r) * pitch + padded, :].astype(bf16)

    for r in range(rows):
        norm_row(r)
    pl.semaphore_wait(barrier, n - 1)
    for side in range(2):
        halo_copy(side).start()
    for copy in loads[2:]:
        copy.wait()
    dec_ref[...] = jnp.transpose(dect_ref[...])

    def lons_of(step):
        return [half + step * rows + r for r in range(rows)]

    def main_loop(step, carry):
        fused(step, lons_of(step), [(half + (step + 1) * rows, rows, 0)])
        send_pairs(step)
        return carry

    lax.fori_loop(0, steps - 2, main_loop, 0)
    for side in range(2):
        halo_copy(side).wait()
    for r in range(half):
        top = (lon_len + half + r) * pitch
        plane_ref[top : top + padded, :] = edge_in[0, r].astype(f32)
        plane_ref[r * pitch : r * pitch + padded, :] = edge_in[1, r].astype(f32)
    fused(steps - 2, lons_of(steps - 2), [(0, half, 0), (lon_len - half, half, half)])
    send_pairs(steps - 2)
    outer = list(range(half)) + list(range(lon_len - half, lon_len))
    tall_ref[...] = jnp.zeros_like(tall_ref)
    term_ref[...] = jnp.zeros_like(term_ref)

    def score_row(step, r, lon):
        at = step * rows + r
        own = own_ref[at].astype(f32)
        misfit = own - observed_ref[pl.ds(lon, own.shape[0], stride=lon_len), :]
        total = misfit * lax.rsqrt(jnp.sum(misfit * misfit, axis=0, keepdims=True) + 1.0)
        pair_sum = jnp.zeros_like(own)
        for k in range(member_n):
            other = own_ref[at] if k == member_n - 1 else others_ref[k, at]
            apart = own - other.astype(f32)
            pair_sum = pair_sum + apart * lax.rsqrt(jnp.sum(apart * apart, axis=0, keepdims=True) + 1.0)
        weight = 4.0 + 8.0 * mask_ref[pl.ds(lon, 1), :].astype(f32)
        score_ref[step, :, r * lat_len : (r + 1) * lat_len] = (
            weight * (total - pair_sum / member_n)
        ).astype(bf16)

    def wait_pairs(step):
        for j in range(member_n - 1):
            pair_copy(step, j).wait()

    def tall_step(step):
        tall_ref[...] += lax.dot_general(
            block_ref[step], score_ref[step], (((1,), (1,)), ((), ())), preferred_element_type=f32
        )

    def score_step(step, lons):
        wait_pairs(step)
        for r in range(rows):
            score_row(step, r, lons[r])
        tall_step(step)

    def grad_step(step, lons):
        grad = jnp.dot(dec_ref[...], score_ref[step], preferred_element_type=f32)
        for r in range(rows):
            plane_ref[pl.ds(lons[r] * pitch, channels), :] = grad[:, r * lat_len : (r + 1) * lat_len]

    def grad_loop(step, carry):
        grad_step(step, lons_of(step))
        return carry

    early = steps - 3
    for step in range(early):
        wait_pairs(step)
    side = []
    for step in range(early):
        side += [functools.partial(score_row, step, r, lons_of(step)[r]) for r in range(rows)]
        side.append(functools.partial(tall_step, step))
    interleave(mlp_pieces(steps - 1, outer), side)
    send_pairs(steps - 1)
    for step in range(early, steps - 1):
        score_step(step, lons_of(step))
    lax.fori_loop(0, steps - 1, grad_loop, 0)
    score_step(steps - 1, outer)
    term_ref[:, 0:channels] = scale * jnp.transpose(tall_ref[...])

    per = mine_sum.shape[0] // 8
    tall = term_ref.shape[0] // 8
    across = term_ref.shape[1] // 128
    for at in range(n * per):
        low = 8 * (at % per)
        if at < tall * across:
            a, b = at // across, at % across
            tile = term_ref[8 * a : 8 * a + 8, 128 * b : 128 * b + 128].astype(bf16)
        else:
            tile = jnp.zeros((8, 128), bf16)
        mine[at // per, low : low + 8, :] = tile

    def scatter_copy(e):
        other, device = peer(e)
        return pltpu.make_async_remote_copy(
            src_ref=mine.at[other], dst_ref=got.at[e], send_sem=sems.at[0, e],
            recv_sem=sems.at[1, e], device_id=device, device_id_type=MESH,
        )

    def gather_copy(e):
        _, device = peer(e)
        return pltpu.make_async_remote_copy(
            src_ref=mine_sum, dst_ref=whole.at[me], send_sem=sems.at[2, e],
            recv_sem=sems.at[3, e], device_id=device, device_id_type=MESH,
        )

    owners = -(-tall * across // per)
    owner = me < owners

    def each(act):
        def body(e, carry):
            act(e)
            return carry

        lax.fori_loop(0, n - 1, body, 0)

    def scatter_start(e):
        pl.when(peer(e)[0] < owners)(lambda: scatter_copy(e).start())

    def scatter_finish(e):
        pl.when(peer(e)[0] < owners)(lambda: scatter_copy(e).wait_send())
        pl.when(owner)(lambda: scatter_copy(e).wait_recv())

    def gather_start(e):
        gather_copy(e).start()

    def gather_finish(e):
        pl.when(owner)(lambda: gather_copy(e).wait_send())
        pl.when(lax.rem(me + n - e - 1, n) < owners)(lambda: gather_copy(e).wait_recv())

    def turn_back(c):
        grad_ref[c] = plane_ref[pl.ds(c, lon_len, stride=pitch), :].astype(bf16)

    def turn_back8(i, carry):
        for k in range(8):
            turn_back(i * 8 + k)
        return carry

    def turn_part(k):
        low, high = parts[k]
        lax.fori_loop(low // 8, high // 8, turn_back8, 0)
        for c in range(high // 8 * 8, high):
            turn_back(c)

    each(scatter_start)
    grad_step(steps - 1, outer)
    first = len(parts) - 1
    for k in range(first):
        turn_part(k)
    each(scatter_finish)

    @pl.when(owner)
    def _():
        total = mine[me].astype(f32)
        for e in range(n - 1):
            total = total + got[e].astype(f32)
        mine_sum[...] = total.astype(bf16)
        each(gather_start)
        whole[me] = mine_sum[...]

    for k in range(first, len(parts)):
        turn_part(k)
    each(gather_finish)
    out_ref[0:owners] = whole[0:owners].astype(f32)
    if owners < n:
        out_ref[owners:n] = jnp.zeros((n - owners, per * 8, 128), f32)


def last_kernel(grad_in, tiles_ref, grad_out, out_ref, flat_ref, sems):
    channels = grad_in.shape[0]
    parts = spans(channels, 128)
    copies = [
        pltpu.make_async_copy(grad_in.at[low:high], grad_out.at[low:high], sems.at[k])
        for k, (low, high) in enumerate(parts)
    ]
    for copy in copies:
        copy.start()
    across = flat_ref.shape[1] // 128
    per = tiles_ref.shape[1] // 8
    for at in range(flat_ref.shape[0] // 8 * across):
        a, b = at // across, at % across
        low = 8 * (at % per)
        flat_ref[8 * a : 8 * a + 8, 128 * b : 128 * b + 128] = tiles_ref[at // per, low : low + 8, :]
    out_ref[...] = flat_ref[:, 0:channels]
    for copy in copies:
        copy.wait()


def per_device(features, depth_kernel, in_weight, out_weight, decoder_weight, observed, land_mask):
    _, channels, lon_len, lat_len = features.shape
    hid = in_weight.shape[1]
    outputs = decoder_weight.shape[1]
    size = depth_kernel.shape[1]
    half = size // 2
    member_n = lax.axis_size("member")
    space_n = lax.axis_size("space")
    n = member_n * space_n
    members = features.shape[0] * member_n
    total_points = lon_len * space_n * lat_len
    padded_c = round_up(channels, 16)
    pitch = padded_c + 1
    wide_c = round_up(channels, 128)
    tiles = (outputs // 8) * (wide_c // 128)
    per = -(-tiles // n)
    rows = 2 * half
    steps = lon_len // rows
    wide = rows * lat_len
    parts = channels // 128
    grad, summed = pl.pallas_call(
        functools.partial(kernel, (member_n, space_n), half, 1.0 / math.sqrt(members * total_points)),
        name="main",
        out_shape=(
            pltpu.VMEM((channels, lon_len, lat_len), bf16),
            pltpu.VMEM((n, per * 8, 128), f32),
        ),
        in_specs=[ANY_SPEC] * 7,
        out_specs=[VMEM_SPEC, VMEM_SPEC],
        scratch_shapes=[
            pltpu.VMEM((channels, lon_len, lat_len), bf16),
            pltpu.VMEM(((lon_len + 2 * half) * pitch, lat_len), f32),
            pltpu.VMEM((size, size, channels), f32),
            pltpu.VMEM((round_up(size * size, 32), wide_c), f32),
            pltpu.VMEM((wide_c, round_up(size * size, 32)), f32),
            pltpu.VMEM((size * size, padded_c, lat_len), f32),
            pltpu.VMEM((channels, hid), bf16),
            pltpu.VMEM((hid, channels), bf16),
            pltpu.VMEM((channels, hid), bf16),
            pltpu.VMEM((outputs, channels), bf16),
            pltpu.VMEM((channels, outputs), bf16),
            pltpu.VMEM((outputs * lon_len, lat_len), f32),
            pltpu.VMEM((lon_len, lat_len), jnp.int32),
            pltpu.VMEM((rows, padded_c, lat_len), f32),
            pltpu.VMEM((channels, wide), bf16),
            pltpu.VMEM((hid, wide), bf16),
            pltpu.VMEM((steps, channels, wide), bf16),
            pltpu.VMEM((lon_len, outputs, lat_len), bf16),
            pltpu.VMEM((member_n - 1, lon_len, outputs, lat_len), bf16),
            pltpu.VMEM((steps, outputs, wide), bf16),
            pltpu.VMEM((channels, outputs), f32),
            pltpu.VMEM((outputs, wide_c), f32),
            pltpu.VMEM((n, per * 8, 128), bf16),
            pltpu.VMEM((n - 1, per * 8, 128), bf16),
            pltpu.VMEM((per * 8, 128), bf16),
            pltpu.VMEM((n, per * 8, 128), bf16),
            pltpu.VMEM((2, half, padded_c, lat_len), bf16),
            pltpu.VMEM((2, half, padded_c, lat_len), bf16),
            pltpu.SemaphoreType.DMA((6,)),
            pltpu.SemaphoreType.DMA((parts,)),
            pltpu.SemaphoreType.DMA((2, 2)),
            pltpu.SemaphoreType.DMA((2, member_n - 1, steps)),
            pltpu.SemaphoreType.DMA((4, n - 1)),
        ],
        compiler_params=pltpu.CompilerParams(
            collective_id=0, has_side_effects=True, vmem_limit_bytes=54 * 1024 * 1024
        ),
    )(
        features[0], jnp.transpose(depth_kernel, (1, 2, 0)), in_weight, out_weight.T, decoder_weight.T,
        observed.reshape(outputs * lon_len, lat_len), land_mask,
    )
    grad_out, out = pl.pallas_call(
        last_kernel,
        name="last",
        out_shape=(
            jax.ShapeDtypeStruct((channels, lon_len, lat_len), bf16),
            jax.ShapeDtypeStruct((outputs, channels), f32),
        ),
        in_specs=[VMEM_SPEC, VMEM_SPEC],
        out_specs=[ANY_SPEC, VMEM_SPEC],
        scratch_shapes=[
            pltpu.VMEM((outputs, wide_c), f32),
            pltpu.SemaphoreType.DMA((len(spans(channels, 128)),)),
        ],
        compiler_params=pltpu.CompilerParams(vmem_limit_bytes=16 * 1024 * 1024),
    )(grad, summed)
    return (grad_out[None], out.T)


def solution(mesh):
    placed = (
        P("member", None, "space", None),
        P(),
        P(),
        P(),
        P(),
        P(None, "space", None),
        P("space", None),
    )
    return jax.shard_map(
        per_device,
        mesh=mesh,
        in_specs=placed,
        out_specs=(P("member", None, "space", None), P()),
        check_vma=False,
    )
```

```python
import functools
import math

import jax
import jax.numpy as jnp
from jax import lax
from jax.experimental import pallas as pl
from jax.experimental.pallas import tpu as pltpu
from jax.sharding import PartitionSpec as P

norm_eps = 1e-05
MESH = pl.DeviceIdType.MESH
VMEM_SPEC = pl.BlockSpec(memory_space=pltpu.VMEM)
ANY_SPEC = pl.BlockSpec(memory_space=pl.ANY)
f32 = jnp.float32
bf16 = jnp.bfloat16


def round_up(value, step):
    return -(-value // step) * step


def spans(total, width):
    return [(at, min(at + width, total)) for at in range(0, total, width)]


def gelu_of_half(u):
    return u * (1.0 + lax.erf(u * (2.0**0.5)))


def pair_tree(terms):
    while len(terms) > 1:
        terms = [
            terms[i] + terms[i + 1] if i + 1 < len(terms) else terms[i]
            for i in range(0, len(terms), 2)
        ]
    return terms[0]


def interleave(main, side):
    total = sum(share for _, share in main)
    done = 0
    given = 0.0
    for piece, share in main:
        piece()
        given += share
        until = len(side) if given >= total else int(round(len(side) * given / total))
        while done < until:
            side[done]()
            done += 1


def kernel(
    groups, half, scale, x_hbm, taps_hbm, w1_hbm, w2_hbm, dect_hbm, observed_hbm, mask_hbm, grad_ref, out_ref,
    x_ref, plane_ref, taps_in, tin_ref, taps_ref, expand_ref, coef_ref, w1n_ref, w1_ref, w2_ref, dect_ref, dec_ref,
    observed_ref, mask_ref, conv_ref, normed_ref, act_ref, block_ref, own_ref, others_ref, score_ref, tall_ref,
    term_ref, mine, got, mine_sum, whole, edge_out, edge_in, load_sems, x_sems, halo_sems, pair_sems, sems,
):
    channels, lon_len, lat_len = x_ref.shape
    hid = w1_ref.shape[0]
    size = 2 * half + 1
    pitch = plane_ref.shape[0] // (lon_len + 2 * half)
    rows = 2 * half
    steps = lon_len // rows
    member_n, space_n = groups
    member = lax.axis_index("member")
    space = lax.axis_index("space")
    n = member_n * space_n
    me = member * space_n + space

    def peer(e):
        other = lax.rem(me + e + 1, n)
        return other, (other // space_n, lax.rem(other, space_n))

    barrier = pltpu.get_barrier_semaphore()

    def greet(e, carry):
        pl.semaphore_signal(barrier, inc=1, device_id=peer(e)[1], device_id_type=MESH)
        return carry

    loads = [
        pltpu.make_async_copy(src, dst, load_sems.at[k])
        for k, (src, dst) in enumerate(
            (
                (w1_hbm, w1n_ref), (taps_hbm, taps_in), (w2_hbm, w2_ref), (dect_hbm, dect_ref),
                (observed_hbm, observed_ref.at[0 : observed_hbm.shape[0]]), (mask_hbm, mask_ref),
            )
        )
    ]
    ends = [128 * k for k in range(1, channels // 128)] + [channels]
    parts = list(zip([0] + ends[:-1], ends))
    x_loads = [
        pltpu.make_async_copy(x_hbm.at[low:high], x_ref.at[low:high], x_sems.at[k])
        for k, (low, high) in enumerate(parts)
    ]
    loads[1].start()
    for copy in x_loads:
        copy.start()
    loads[0].start()
    for copy in loads[2:]:
        copy.start()
    lax.fori_loop(0, n - 1, greet, 0)

    loads[1].wait()
    tin_ref[...] = jnp.zeros_like(tin_ref)
    for p in range(size):
        tin_ref[size * p : size * (p + 1), 0:channels] = taps_in[p]
    taps_ref[...] = jnp.transpose(tin_ref[...])
    chunks = -(-channels // 16)

    tap_row = lax.broadcasted_iota(jnp.int32, (expand_ref.shape[0], lat_len), 0)
    tap_lane = lax.broadcasted_iota(jnp.int32, (expand_ref.shape[0], lat_len), 1)
    for at in range(size * size):
        shift = half - at % size
        ok = (tap_row == at) & (tap_lane >= shift) & (tap_lane < lat_len + shift)
        expand_ref[:, at * lat_len : (at + 1) * lat_len] = jnp.where(ok, 1.0, 0.0).astype(bf16)

    def spread(first, groups=1):
        tap = taps_ref[pl.ds(first, 16 * groups), :].astype(bf16)
        wide = jnp.dot(tap, expand_ref[...], preferred_element_type=f32)

        def source_of(part):
            def one(p, q):
                at = p * size + q
                own = wide[16 * part : 16 * part + 16, at * lat_len : (at + 1) * lat_len]
                coef_ref[at, pl.ds(first + 16 * part, 16), :] = own
                return own.astype(bf16)

            return one

        return [source_of(part) for part in range(groups)]

    def kept(first):
        here = pl.ds(first, 16)
        return lambda p, q: coef_ref[p * size + q, here, :].astype(bf16)

    spare = pitch - channels
    for r in range(lon_len + 2 * half):
        plane_ref[r * pitch + channels : (r + 1) * pitch, :] = jnp.zeros((spare, lat_len), f32)

    def turn(c):
        plane_ref[pl.ds(half * pitch + c, lon_len, stride=pitch), :] = x_ref[c].astype(f32)

    def conv_chunk(first, runs, coef_of=None):
        coef_of = coef_of or kept(first)
        cells = {}
        sums = {}
        for base, count, slot in runs:
            for k in range(count + 2 * half):
                cells[slot, k] = plane_ref[pl.ds((base + k) * pitch + first, 16), :].astype(bf16)
        for q in range(size):
            coef = [coef_of(p, q) for p in range(size)]
            for base, count, slot in runs:
                moved = [
                    cells[slot, k] if q == half else pltpu.roll(cells[slot, k], (half - q) % lat_len, 1)
                    for k in range(count + 2 * half)
                ]
                for o in range(count):
                    part = pair_tree([coef[p] * moved[o + p] for p in range(size)])
                    sums.setdefault(slot + o, []).append(part)
        for o, terms in sums.items():
            conv_ref[o, pl.ds(first, 16), :] = pair_tree(terms).astype(f32)

    inner = [(half, rows, 0)]

    def turn16(i):
        for k in range(16):
            turn(i * 16 + k)

    def head(i, carry):
        begin = pl.multiple_of(i * 32 - 32, 16)
        for part, source in enumerate(spread(begin, 2)):
            conv_chunk(begin + 16 * part, inner, source)
        for part in range(2):
            turn16(i * 2 + part)
        return carry

    for k, (low, high) in enumerate(parts):
        x_loads[k].wait()
        if k == 0:
            turn16(0)
            turn16(1)
        lax.fori_loop(max(low // 32, 1), high // 32, head, 0)
    for c in range(channels // 32 * 32, channels):
        turn(c)
    for at in range(channels // 32 * 2 - 2, chunks):
        conv_chunk(16 * at, inner, spread(16 * at)[0])
    loads[0].wait()
    for low, high in spans(hid, 256):
        w1_ref[low:high, :] = jnp.transpose(w1n_ref[:, low:high])

    def conv_pieces(runs):
        return [functools.partial(conv_chunk, 16 * k, runs) for k in range(chunks)]

    def norm_row(r):
        cells = conv_ref[r, 0:channels, :]
        shifted = cells - jnp.sum(cells, axis=0, keepdims=True) * (1.0 / channels)
        square = jnp.sum(shifted * shifted, axis=0, keepdims=True)
        factor = 0.5 * lax.rsqrt(square * (1.0 / channels) + norm_eps)
        normed_ref[:, r * lat_len : (r + 1) * lat_len] = (shifted * factor).astype(bf16)

    def pre_piece():
        pre = jnp.dot(w1_ref[...], normed_ref[...], preferred_element_type=f32)
        act_ref[...] = gelu_of_half(pre).astype(bf16)

    def out_piece(step, lons):
        held = jnp.concatenate([plane_ref[pl.ds((lon + half) * pitch, channels), :] for lon in lons], axis=1)
        out = held + jnp.dot(w2_ref[...], act_ref[...], preferred_element_type=f32)
        block_ref[step] = out.astype(bf16)

    def decode_piece(step):
        decoded = jnp.dot(dect_ref[...], block_ref[step], preferred_element_type=f32).astype(bf16)
        for r in range(rows):
            own_ref[step * rows + r] = decoded[:, r * lat_len : (r + 1) * lat_len]

    def mlp_pieces(step, lons):
        return [
            (pre_piece, 15.0), (functools.partial(out_piece, step, lons), 27.0),
            (functools.partial(decode_piece, step), 1.0),
        ]

    def fused(step, lons, runs):
        norms = [functools.partial(norm_row, r) for r in range(rows)]
        interleave(mlp_pieces(step, lons), conv_pieces(runs) + norms)

    def pair_copy(step, j):
        at = pl.ds(step * rows, rows)
        return pltpu.make_async_remote_copy(
            src_ref=own_ref.at[at], dst_ref=others_ref.at[j, at],
            send_sem=pair_sems.at[0, j, step], recv_sem=pair_sems.at[1, j, step],
            device_id=(lax.rem(member + j + 1, member_n), space), device_id_type=MESH,
        )

    def send_pairs(step):
        for j in range(member_n - 1):
            pair_copy(step, j).start()

    def halo_copy(side):
        to = lax.rem(space + (space_n - 1 if side == 0 else 1), space_n)
        return pltpu.make_async_remote_copy(
            src_ref=edge_out.at[side], dst_ref=edge_in.at[side], send_sem=halo_sems.at[0, side],
            recv_sem=halo_sems.at[1, side], device_id=(member, to), device_id_type=MESH,
        )

    padded = edge_out.shape[2]
    for r in range(half):
        edge_out[0, r] = plane_ref[(half + r) * pitch : (half + r) * pitch + padded, :].astype(bf16)
        edge_out[1, r] = plane_ref[(lon_len + r) * pitch : (lon_len + r) * pitch + padded, :].astype(bf16)

    for r in range(rows):
        norm_row(r)
    pl.semaphore_wait(barrier, n - 1)
    for side in range(2):
        halo_copy(side).start()
    for copy in loads[2:]:
        copy.wait()
    dec_ref[...] = jnp.transpose(dect_ref[...])

    def lons_of(step):
        return [half + step * rows + r for r in range(rows)]

    def main_loop(step, carry):
        fused(step, lons_of(step), [(half + (step + 1) * rows, rows, 0)])
        send_pairs(step)
        return carry

    lax.fori_loop(0, steps - 2, main_loop, 0)
    for side in range(2):
        halo_copy(side).wait()
    for r in range(half):
        top = (lon_len + half + r) * pitch
        plane_ref[top : top + padded, :] = edge_in[0, r].astype(f32)
        plane_ref[r * pitch : r * pitch + padded, :] = edge_in[1, r].astype(f32)
    fused(steps - 2, lons_of(steps - 2), [(0, half, 0), (lon_len - half, half, half)])
    send_pairs(steps - 2)
    outer = list(range(half)) + list(range(lon_len - half, lon_len))
    tall_ref[...] = jnp.zeros_like(tall_ref)
    term_ref[...] = jnp.zeros_like(term_ref)

    def score_row(step, r, lon):
        at = step * rows + r
        own = own_ref[at].astype(f32)
        misfit = own - observed_ref[pl.ds(lon, own.shape[0], stride=lon_len), :]
        total = misfit * lax.rsqrt(jnp.sum(misfit * misfit, axis=0, keepdims=True) + 1.0)
        pair_sum = jnp.zeros_like(own)
        for k in range(member_n):
            other = own_ref[at] if k == member_n - 1 else others_ref[k, at]
            apart = own - other.astype(f32)
            pair_sum = pair_sum + apart * lax.rsqrt(jnp.sum(apart * apart, axis=0, keepdims=True) + 1.0)
        weight = 4.0 + 8.0 * mask_ref[pl.ds(lon, 1), :].astype(f32)
        score_ref[step, :, r * lat_len : (r + 1) * lat_len] = (
            weight * (total - pair_sum / member_n)
        ).astype(bf16)

    def wait_pairs(step):
        for j in range(member_n - 1):
            pair_copy(step, j).wait()

    def tall_step(step):
        tall_ref[...] += lax.dot_general(
            block_ref[step], score_ref[step], (((1,), (1,)), ((), ())), preferred_element_type=f32
        )

    def score_step(step, lons):
        wait_pairs(step)
        for r in range(rows):
            score_row(step, r, lons[r])
        tall_step(step)

    def grad_step(step, lons):
        grad = jnp.dot(dec_ref[...], score_ref[step], preferred_element_type=f32)
        for r in range(rows):
            plane_ref[pl.ds(lons[r] * pitch, channels), :] = grad[:, r * lat_len : (r + 1) * lat_len]

    def grad_loop(step, carry):
        grad_step(step, lons_of(step))
        return carry

    early = steps - 3
    for step in range(early):
        wait_pairs(step)
    side = []
    for step in range(early):
        side += [functools.partial(score_row, step, r, lons_of(step)[r]) for r in range(rows)]
        side.append(functools.partial(tall_step, step))
    interleave(mlp_pieces(steps - 1, outer), side)
    send_pairs(steps - 1)
    for step in range(early, steps - 1):
        score_step(step, lons_of(step))
    lax.fori_loop(0, steps - 1, grad_loop, 0)
    score_step(steps - 1, outer)
    term_ref[:, 0:channels] = scale * jnp.transpose(tall_ref[...])

    per = mine_sum.shape[0] // 8
    tall = term_ref.shape[0] // 8
    across = term_ref.shape[1] // 128
    for at in range(n * per):
        low = 8 * (at % per)
        if at < tall * across:
            a, b = at // across, at % across
            tile = term_ref[8 * a : 8 * a + 8, 128 * b : 128 * b + 128].astype(bf16)
        else:
            tile = jnp.zeros((8, 128), bf16)
        mine[at // per, low : low + 8, :] = tile

    def scatter_copy(e):
        other, device = peer(e)
        return pltpu.make_async_remote_copy(
            src_ref=mine.at[other], dst_ref=got.at[e], send_sem=sems.at[0, e],
            recv_sem=sems.at[1, e], device_id=device, device_id_type=MESH,
        )

    def gather_copy(e):
        _, device = peer(e)
        return pltpu.make_async_remote_copy(
            src_ref=mine_sum, dst_ref=whole.at[me], send_sem=sems.at[2, e],
            recv_sem=sems.at[3, e], device_id=device, device_id_type=MESH,
        )

    owners = -(-tall * across // per)
    owner = me < owners

    def each(act):
        def body(e, carry):
            act(e)
            return carry

        lax.fori_loop(0, n - 1, body, 0)

    def scatter_start(e):
        pl.when(peer(e)[0] < owners)(lambda: scatter_copy(e).start())

    def scatter_finish(e):
        pl.when(peer(e)[0] < owners)(lambda: scatter_copy(e).wait_send())
        pl.when(owner)(lambda: scatter_copy(e).wait_recv())

    def gather_start(e):
        gather_copy(e).start()

    def gather_finish(e):
        pl.when(owner)(lambda: gather_copy(e).wait_send())
        pl.when(lax.rem(me + n - e - 1, n) < owners)(lambda: gather_copy(e).wait_recv())

    def turn_back(c):
        grad_ref[c] = plane_ref[pl.ds(c, lon_len, stride=pitch), :].astype(bf16)

    def turn_back8(i, carry):
        for k in range(8):
            turn_back(i * 8 + k)
        return carry

    def turn_part(k):
        low, high = parts[k]
        lax.fori_loop(low // 8, high // 8, turn_back8, 0)
        for c in range(high // 8 * 8, high):
            turn_back(c)

    each(scatter_start)
    grad_step(steps - 1, outer)
    first = len(parts) - 1
    for k in range(first):
        turn_part(k)
    each(scatter_finish)

    @pl.when(owner)
    def _():
        total = mine[me].astype(f32)
        for e in range(n - 1):
            total = total + got[e].astype(f32)
        mine_sum[...] = total.astype(bf16)
        each(gather_start)
        whole[me] = mine_sum[...]

    for k in range(first, len(parts)):
        turn_part(k)
    each(gather_finish)
    out_ref[0:owners] = whole[0:owners].astype(f32)
    if owners < n:
        out_ref[owners:n] = jnp.zeros((n - owners, per * 8, 128), f32)


def last_kernel(grad_in, tiles_ref, grad_out, out_ref, flat_ref, sems):
    channels = grad_in.shape[0]
    parts = spans(channels, 128)
    copies = [
        pltpu.make_async_copy(grad_in.at[low:high], grad_out.at[low:high], sems.at[k])
        for k, (low, high) in enumerate(parts)
    ]
    for copy in copies:
        copy.start()
    across = flat_ref.shape[1] // 128
    per = tiles_ref.shape[1] // 8
    for at in range(flat_ref.shape[0] // 8 * across):
        a, b = at // across, at % across
        low = 8 * (at % per)
        flat_ref[8 * a : 8 * a + 8, 128 * b : 128 * b + 128] = tiles_ref[at // per, low : low + 8, :]
    out_ref[...] = flat_ref[:, 0:channels]
    for copy in copies:
        copy.wait()


def per_device(features, depth_kernel, in_weight, out_weight, decoder_weight, observed, land_mask):
    _, channels, lon_len, lat_len = features.shape
    hid = in_weight.shape[1]
    outputs = decoder_weight.shape[1]
    size = depth_kernel.shape[1]
    half = size // 2
    member_n = lax.axis_size("member")
    space_n = lax.axis_size("space")
    n = member_n * space_n
    members = features.shape[0] * member_n
    total_points = lon_len * space_n * lat_len
    padded_c = round_up(channels, 16)
    pitch = padded_c + 1
    wide_c = round_up(channels, 128)
    tiles = (outputs // 8) * (wide_c // 128)
    per = -(-tiles // n)
    rows = 2 * half
    steps = lon_len // rows
    wide = rows * lat_len
    parts = channels // 128
    grad, summed = pl.pallas_call(
        functools.partial(kernel, (member_n, space_n), half, 1.0 / math.sqrt(members * total_points)),
        name="main",
        out_shape=(
            pltpu.VMEM((channels, lon_len, lat_len), bf16),
            pltpu.VMEM((n, per * 8, 128), f32),
        ),
        in_specs=[ANY_SPEC] * 7,
        out_specs=[VMEM_SPEC, VMEM_SPEC],
        scratch_shapes=[
            pltpu.VMEM((channels, lon_len, lat_len), bf16),
            pltpu.VMEM(((lon_len + 2 * half) * pitch, lat_len), f32),
            pltpu.VMEM((size, size, channels), f32),
            pltpu.VMEM((round_up(size * size, 32), wide_c), f32),
            pltpu.VMEM((wide_c, round_up(size * size, 32)), f32),
            pltpu.VMEM((round_up(size * size, 32), size * size * lat_len), bf16),
            pltpu.VMEM((size * size, padded_c, lat_len), f32),
            pltpu.VMEM((channels, hid), bf16),
            pltpu.VMEM((hid, channels), bf16),
            pltpu.VMEM((channels, hid), bf16),
            pltpu.VMEM((outputs, channels), bf16),
            pltpu.VMEM((channels, outputs), bf16),
            pltpu.VMEM(((outputs + 1) * lon_len, lat_len), f32),
            pltpu.VMEM((lon_len, lat_len), jnp.int32),
            pltpu.VMEM((rows, padded_c, lat_len), f32),
            pltpu.VMEM((channels, wide), bf16),
            pltpu.VMEM((hid, wide), bf16),
            pltpu.VMEM((steps, channels, wide), bf16),
            pltpu.VMEM((lon_len, outputs, lat_len), bf16),
            pltpu.VMEM((member_n - 1, lon_len, outputs, lat_len), bf16),
            pltpu.VMEM((steps, outputs, wide), bf16),
            pltpu.VMEM((channels, outputs), f32),
            pltpu.VMEM((outputs, wide_c), f32),
            pltpu.VMEM((n, per * 8, 128), bf16),
            pltpu.VMEM((n - 1, per * 8, 128), bf16),
            pltpu.VMEM((per * 8, 128), bf16),
            pltpu.VMEM((n, per * 8, 128), bf16),
            pltpu.VMEM((2, half, padded_c, lat_len), bf16),
            pltpu.VMEM((2, half, padded_c, lat_len), bf16),
            pltpu.SemaphoreType.DMA((6,)),
            pltpu.SemaphoreType.DMA((parts,)),
            pltpu.SemaphoreType.DMA((2, 2)),
            pltpu.SemaphoreType.DMA((2, member_n - 1, steps)),
            pltpu.SemaphoreType.DMA((4, n - 1)),
        ],
        compiler_params=pltpu.CompilerParams(
            collective_id=0, has_side_effects=True, vmem_limit_bytes=54 * 1024 * 1024
        ),
    )(
        features[0], jnp.transpose(depth_kernel, (1, 2, 0)), in_weight, out_weight.T, decoder_weight.T,
        observed.reshape(outputs * lon_len, lat_len), land_mask,
    )
    grad_out, out = pl.pallas_call(
        last_kernel,
        name="last",
        out_shape=(
            jax.ShapeDtypeStruct((channels, lon_len, lat_len), bf16),
            jax.ShapeDtypeStruct((outputs, channels), f32),
        ),
        in_specs=[VMEM_SPEC, VMEM_SPEC],
        out_specs=[ANY_SPEC, VMEM_SPEC],
        scratch_shapes=[
            pltpu.VMEM((outputs, wide_c), f32),
            pltpu.SemaphoreType.DMA((len(spans(channels, 128)),)),
        ],
        compiler_params=pltpu.CompilerParams(vmem_limit_bytes=16 * 1024 * 1024),
    )(grad, summed)
    return (grad_out[None], out.T)


def solution(mesh):
    placed = (
        P("member", None, "space", None),
        P(),
        P(),
        P(),
        P(),
        P(None, "space", None),
        P("space", None),
    )
    return jax.shard_map(
        per_device,
        mesh=mesh,
        in_specs=placed,
        out_specs=(P("member", None, "space", None), P()),
        check_vma=False,
    )
```
